768 devices in a mesh: fsdp: 192 (over z, y, core), row: 4 (over x).
Axes of the slice: x: 4, y: 8, z: 12, core: 2. Of those that a mesh axis runs over, the one named last changes fastest.
Arguments:
- factor: float32 [3072, 3072], P('fsdp', 'row'), may hold values from -1 to 17, as said below
- gradient: bfloat16 [3072, 3840], P('row', 'fsdp'), may hold values from -0.125 to 0.125
- sketch_ids: int32 [3072, 256], P('row'), may hold values from -3 to 3
Outputs:
- factor_new: float32 [3072, 3072], P('fsdp', 'row')
- range_basis: float32 [3072, 256], P('fsdp')
- projected_core: float32 [256, 256], replicated
The draws below stay inside these ranges and needn't reach their ends.
Inputs may be any that keep to these rules, and one draw needn't show every extreme that they name: `factor`: symmetric.
All inputs are finite; a program needn't handle non-finite values.
Results may differ from the reference program's by a relative error of at most 0.0003.
Values may be sent and summed in bfloat16 or wider, within the bound.
No kernel may reach another device: no remote copies, remote signals or barrier semaphores. Data moves between devices by JAX's collectives and lax.ppermute only.
A program may use at most 64 MiB of HBM per device.

```python
import math
import jax
import jax.numpy as jnp
from jax import lax

B = 3072
C = 3840
R = 256


def draw_factor(key, part):
    first_key, second_key = jax.random.split(key)
    diagonal_part = jnp.exp(jax.random.uniform(first_key, (B,), jnp.float32, math.log(2.0), math.log(16.0)))
    spread = 2.0
    noise_field = jax.random.uniform(second_key, (B, B), jnp.float32, -1.0, 1.0) * (spread / B ** 0.5)
    symmetric = 0.5 * (noise_field + noise_field.T)
    return jnp.eye(B, dtype=jnp.float32) * diagonal_part[:, None] + symmetric


def set_ends(result, key, smallest, high):
    extent = result.shape
    place = [jax.random.randint(jax.random.fold_in(key, axis), (), 0, extent[axis]) for axis in range(len(extent))]
    result = result.at[tuple(place)].set(smallest)
    longest = extent.index(max(extent))
    place[longest] = (place[longest] + 1) % extent[longest]
    return result.at[tuple(place)].set(high)


def shard_levels(own_key, extent, cuts, least, largest):
    def one(axis_at, blocks):
        draws = jax.random.uniform(jax.random.fold_in(jax.random.fold_in(own_key, 6), axis_at), (blocks,), jnp.float32, least / len(cuts), largest / len(cuts))
        return jnp.repeat(jnp.exp(draws), extent[axis_at] // blocks).reshape((-1,) + (1,) * (len(extent) - axis_at - 1))

    level = one(*cuts[0])
    for cut in cuts[1:]:
        level = level * one(*cut)
    return level


def centred(key, shape, scale, reach, shards=(), kind=jnp.bfloat16):
    array = jax.random.normal(key, shape, jnp.float32) * scale
    if len(shards) > 0:
        array = shard_levels(key, shape, shards, -0.22, 0.18) * array
    return jnp.clip(array, min=-reach, max=reach).astype(kind)


def setup_inputs(seed: int = 0) -> dict:
    streams_of = jax.random.split(jax.random.key(seed), 4)
    factor = draw_factor(jax.random.fold_in(streams_of[3], 71), 0)
    gradient = centred(streams_of[1], (B, C), (C // 2) ** -0.5, 0.125, ((0, 4), (1, 192)))
    sketch_ids = set_ends(jax.random.randint(streams_of[2], (B, R), -3, 4), jax.random.fold_in(streams_of[2], 1), -3, 3).astype(jnp.int32)
    return dict(factor=factor, gradient=gradient, sketch_ids=sketch_ids)


decay_rate = 0.9

def reference(factor, gradient, sketch_ids):
    highest = lax.Precision.HIGHEST
    outer_sum = jnp.dot(gradient.astype(jnp.float32), gradient.T.astype(jnp.float32), preferred_element_type=jnp.float32)
    factor_new = decay_rate * factor + outer_sum
    sketch = sketch_ids.astype(jnp.float32)
    ranged = jnp.dot(factor_new, sketch, precision=highest)
    gram_matrix = jnp.dot(ranged.T, ranged, precision=highest) / B
    lower_factor = jnp.linalg.cholesky(gram_matrix)
    range_basis = jax.scipy.linalg.solve_triangular(lower_factor, ranged.T, lower=True).T
    applied = jnp.dot(factor_new, range_basis, precision=highest)
    projected_core = jnp.dot(range_basis.T, applied, precision=highest) / B
    return (factor_new, range_basis, projected_core)
```

```python
import jax
import jax.numpy as jnp
from jax import lax
from jax.sharding import Mesh, PartitionSpec as P

B = 3072
decay_rate = 0.9
NZ, NY, NC, NX = 12, 8, 2, 4
ALL = ("z", "y", "c", "x")
F32 = jnp.float32
HI = lax.Precision.HIGHEST


def dot(a, b, ca, cb):
    return lax.dot_general(a, b, (((ca,), (cb,)), ((), ())), precision=HI, preferred_element_type=F32)


def spread(v, axis, n):
    return lax.all_to_all(jnp.broadcast_to(v[None], (n,) + v.shape), axis, 0, 0)


def swap_core(v):
    return lax.ppermute(v, "c", [(0, 1), (1, 0)])


def scatter_core(v, core):
    half = v.shape[0] // 2
    mine = lax.dynamic_slice_in_dim(v, core * half, half, 0)
    other = lax.dynamic_slice_in_dim(v, (1 - core) * half, half, 0)
    return mine + swap_core(other)


def scatter(v, axis, n):
    return jnp.sum(lax.all_to_all(v.reshape(n, v.shape[0] // n, v.shape[1]), axis, 0, 0), axis=0)


def join(v):
    return v.reshape(v.shape[0] * v.shape[1], v.shape[2])


def shards(factor, gradient, sketch_ids):
    rows, cols = factor.shape
    z, y, c, x = (lax.axis_index(a) for a in ALL)
    owner = z // (NZ // NX)
    offset = rows * (((z % (NZ // NX)) * NY + y) * NC + c)
    mine = (x == owner).astype(F32)

    strip = jnp.pad(gradient.T, ((0, 4), (0, 0)))
    plane = lax.all_gather(strip, ("z", "y"), axis=0, tiled=False)

    grad32 = gradient.astype(F32)
    sketch = sketch_ids.astype(F32)
    small = jnp.concatenate([dot(grad32, sketch, 0, 0), decay_rate * dot(factor, sketch, 1, 0)], axis=0)
    small = jnp.sum(spread(small, "x", NX), axis=0)
    inner, decayed = small[:gradient.shape[1]], small[gradient.shape[1]:]
    place = (lax.broadcasted_iota(jnp.int32, (cols, rows), 0) == offset + lax.broadcasted_iota(jnp.int32, (cols, rows), 1)).astype(F32)
    partial = dot(jnp.concatenate([grad32, mine * place], axis=1), jnp.concatenate([inner, decayed], axis=0), 1, 0)
    piece = scatter(scatter(scatter_core(partial, c), "y", NY), "z", NZ)
    piece = join(spread(join(spread(piece, "z", NZ)), "y", NY))
    ranged = lax.all_gather(piece, "c", axis=0, tiled=True)

    here = mine * lax.dynamic_slice_in_dim(ranged, offset, rows, 0)
    gram = dot(lax.dynamic_slice_in_dim(ranged, c * 128, 128, 1), ranged, 0, 0)
    part = jnp.concatenate([gram, dot(grad32, ranged, 0, 0), here], axis=0)
    part = jnp.sum(spread(part, "x", NX), axis=0)
    gram, weighted, own_rows = part[:128], part[128:128 + gradient.shape[1]], part[128 + gradient.shape[1]:]
    gram_matrix = lax.all_gather(gram, "c", axis=0, tiled=True) / B

    core = decay_rate * dot(own_rows, dot(factor, ranged, 1, 0), 0, 0)
    core = core + (x == 0).astype(F32) * dot(weighted, weighted, 0, 0)
    core = scatter(scatter_core(core, c), ("y", "x"), NY * NX)
    core = jnp.sum(spread(core, "z", NZ), axis=0)
    core = join(spread(core, ("y", "x"), NY * NX))
    core = lax.all_gather(core, "c", axis=0, tiled=True)

    lower_factor = jnp.linalg.cholesky(gram_matrix)
    inverse = jax.scipy.linalg.solve_triangular(lower_factor, jnp.eye(256, dtype=F32), lower=True)
    range_basis = dot(own_rows, inverse, 1, 1)
    projected_core = dot(dot(inverse, core, 1, 0), inverse, 1, 1) / B

    plane, _ = lax.optimization_barrier((plane, inverse))
    plane = plane.reshape(-1, cols)
    plane = lax.all_gather(plane, "c", axis=0, tiled=True)
    picked = lax.dot_general(place.astype(jnp.bfloat16), plane, (((0,), (1,)), ((), ())), preferred_element_type=F32).astype(jnp.bfloat16)
    picked = picked * mine.astype(jnp.bfloat16)
    total = picked
    for k in range(1, NX):
        pairs = []
        for d in range(NZ * NY * NC):
            src = (d // (NY * NC)) // (NZ // NX)
            pairs.append((d * NX + src, d * NX + (src + k) % NX))
        total = total + lax.ppermute(picked, ALL, pairs)
    outer_sum = lax.dot_general(total, plane, (((1,), (0,)), ((), ())), preferred_element_type=F32)
    factor_new = decay_rate * factor + outer_sum
    return (factor_new, range_basis, projected_core)


def solution(mesh):
    fine = Mesh(mesh.devices.reshape(NZ, NY, NC, NX), ALL)
    f = ("z", "y", "c")
    return jax.shard_map(
        shards,
        mesh=fine,
        in_specs=(P(f, "x"), P("x", f), P("x", None)),
        out_specs=(P(f, "x"), P(f, None), P()),
        check_vma=False,
    )
```

```python
import jax
import jax.numpy as jnp
from jax import lax
from jax.sharding import Mesh, PartitionSpec as P

B = 3072
decay_rate = 0.9
NZ, NY, NC, NX = 12, 8, 2, 4
ALL = ("z", "y", "c", "x")
F32 = jnp.float32
HI = lax.Precision.HIGHEST


def dot(a, b, ca, cb):
    return lax.dot_general(a, b, (((ca,), (cb,)), ((), ())), precision=HI, preferred_element_type=F32)


def spread(v, axis, n):
    return lax.all_to_all(jnp.broadcast_to(v[None], (n,) + v.shape), axis, 0, 0)


def swap_core(v):
    return lax.ppermute(v, "c", [(0, 1), (1, 0)])


def scatter_core(v, core):
    half = v.shape[0] // 2
    mine = lax.dynamic_slice_in_dim(v, core * half, half, 0)
    other = lax.dynamic_slice_in_dim(v, (1 - core) * half, half, 0)
    return mine + swap_core(other)


def scatter(v, axis, n):
    return jnp.sum(lax.all_to_all(v.reshape(n, v.shape[0] // n, v.shape[1]), axis, 0, 0), axis=0)


def join(v):
    return v.reshape(v.shape[0] * v.shape[1], v.shape[2])


def shards(factor, gradient, sketch_ids):
    rows, cols = factor.shape
    z, y, c, x = (lax.axis_index(a) for a in ALL)
    owner = z // (NZ // NX)
    offset = rows * (((z % (NZ // NX)) * NY + y) * NC + c)
    mine = (x == owner).astype(F32)

    strip = jnp.pad(gradient.T, ((0, 4), (0, 0)))
    plane = lax.all_gather(strip, ("z", "y", "c"), axis=0, tiled=True)

    grad32 = gradient.astype(F32)
    sketch = sketch_ids.astype(F32)
    small = jnp.concatenate([dot(grad32, sketch, 0, 0), decay_rate * dot(factor, sketch, 1, 0)], axis=0)
    small = jnp.sum(spread(small, "x", NX), axis=0)
    inner, decayed = small[:gradient.shape[1]], small[gradient.shape[1]:]
    place = (lax.broadcasted_iota(jnp.int32, (cols, rows), 0) == offset + lax.broadcasted_iota(jnp.int32, (cols, rows), 1)).astype(F32)
    partial = dot(jnp.concatenate([grad32, mine * place], axis=1), jnp.concatenate([inner, decayed], axis=0), 1, 0)
    piece = scatter(scatter_core(partial, c), ("z", "y"), NZ * NY)
    piece = join(spread(piece, ("z", "y"), NZ * NY))
    ranged = lax.all_gather(piece, "c", axis=0, tiled=True)

    here = mine * lax.dynamic_slice_in_dim(ranged, offset, rows, 0)
    gram = dot(lax.dynamic_slice_in_dim(ranged, c * 128, 128, 1), ranged, 0, 0)
    wide = gradient.shape[1]
    part = jnp.concatenate([gram, here, dot(grad32, ranged, 0, 0), decay_rate * dot(factor, ranged, 1, 0)], axis=0)
    part = jnp.sum(spread(part, "x", NX), axis=0)
    gram, own_rows = part[:128], part[128:128 + rows]
    left = part[128:128 + rows + wide]
    gram_matrix = lax.all_gather(gram, "c", axis=0, tiled=True) / B

    right = jnp.concatenate([part[128 + rows + wide:], part[128 + rows:128 + rows + wide]], axis=0)
    core = dot(left, right, 0, 0).reshape(NC, NX, 32, 256)
    core = lax.dynamic_index_in_dim(core, x, 1, keepdims=False).reshape(64, 256)
    core = scatter(scatter_core(core, c), "y", NY)
    core = jnp.sum(spread(core, "z", NZ), axis=0)
    core = join(spread(core, ("x", "y"), NX * NY))
    core = lax.all_gather(core, "c", axis=0, tiled=True)

    lower_factor = jnp.linalg.cholesky(gram_matrix)
    inverse = jax.scipy.linalg.solve_triangular(lower_factor, jnp.eye(256, dtype=F32), lower=True)
    range_basis = dot(own_rows, inverse, 1, 1)
    projected_core = dot(dot(inverse, core, 1, 0), inverse, 1, 1) / B

    late = (lower_factor[0, 0] > 0).astype(jnp.int32) >> 1
    place = (lax.broadcasted_iota(jnp.int32, (cols, rows), 0) == offset + late + lax.broadcasted_iota(jnp.int32, (cols, rows), 1))
    picked = lax.dot_general(place.astype(jnp.bfloat16), plane, (((0,), (1,)), ((), ())), preferred_element_type=F32).astype(jnp.bfloat16)
    picked = picked * mine.astype(jnp.bfloat16)
    total = picked
    for k in range(1, NX):
        pairs = []
        for d in range(NZ * NY * NC):
            src = (d // (NY * NC)) // (NZ // NX)
            pairs.append((d * NX + src, d * NX + (src + k) % NX))
        total = total + lax.ppermute(picked, ALL, pairs)
    outer_sum = lax.dot_general(total, plane, (((1,), (0,)), ((), ())), preferred_element_type=F32)
    factor_new = decay_rate * factor + outer_sum
    return (factor_new, range_basis, projected_core)


def solution(mesh):
    fine = Mesh(mesh.devices.reshape(NZ, NY, NC, NX), ALL)
    f = ("z", "y", "c")
    return jax.shard_map(
        shards,
        mesh=fine,
        in_specs=(P(f, "x"), P("x", f), P("x", None)),
        out_specs=(P(f, "x"), P(f, None), P()),
        check_vma=False,
    )
```

```python
import jax
import jax.numpy as jnp
from jax import lax
from jax.experimental import pallas as pl
from jax.experimental.pallas import tpu as pltpu
from jax.sharding import Mesh, PartitionSpec as P

B = 3072
decay_rate = 0.9
NZ, NY, NC, NX = 12, 8, 2, 4
ALL = ("z", "y", "c", "x")
F32 = jnp.float32
BF16 = jnp.bfloat16
R, PANEL, GROUP, LANES = 256, 32, 8, 128
HI = lax.Precision.HIGHEST


def dot(a, b, ca, cb):
    return lax.dot_general(a, b, (((ca,), (cb,)), ((), ())), precision=HI, preferred_element_type=F32)


def spread(v, axis, n):
    return lax.all_to_all(jnp.broadcast_to(v[None], (n,) + v.shape), axis, 0, 0)


def swap_core(v):
    return lax.ppermute(v, "c", [(0, 1), (1, 0)])


def scatter_core(v, core):
    half = v.shape[0] // 2
    mine = lax.dynamic_slice_in_dim(v, core * half, half, 0)
    other = lax.dynamic_slice_in_dim(v, (1 - core) * half, half, 0)
    return mine + swap_core(other)


def scatter(v, axis, n):
    return jnp.sum(lax.all_to_all(v.reshape(n, v.shape[0] // n, v.shape[1]), axis, 0, 0), axis=0)


def join(v):
    return v.reshape(v.shape[0] * v.shape[1], v.shape[2])


def split3(v):
    high = v.astype(BF16); rest = v - high.astype(F32)
    mid = rest.astype(BF16)
    return high, mid, (rest - mid.astype(F32)).astype(BF16)


def panel_step(k, a_ref, x_ref, inv_ref):
    tile = k * PANEL // LANES
    rows = slice(k * PANEL, (k + 1) * PANEL)
    n_a = 2 - tile
    w = [a_ref[rows, t * LANES:(t + 1) * LANES] for t in range(tile, 2)]
    w += [x_ref[rows, t * LANES:(t + 1) * LANES] for t in range(tile + 1)]
    lane0 = k * PANEL - tile * LANES
    row = lax.broadcasted_iota(jnp.int32, (PANEL, LANES), 0)
    pivots = jnp.ones((PANEL, LANES), F32)
    for g in range(PANEL // GROUP):
        cols = [jnp.broadcast_to(w[0][:, lane0 + g * GROUP + j:lane0 + g * GROUP + j + 1], (PANEL, LANES)) for j in range(GROUP)]
        for j in range(GROUP):
            at = g * GROUP + j
            pivot = cols[j][at:at + 1, :]
            factor = jnp.where(row > at, cols[j] * (1.0 / pivot), 0.0)
            for t in range(j + 1, GROUP):
                cols[t] = cols[t] - factor * cols[t][at:at + 1, :]
            w = [v - factor * v[at:at + 1, :] for v in w]
            pivots = jnp.where(row == at, pivot, pivots)
    scale = lax.rsqrt(pivots)
    w = [v * scale for v in w]
    for t in range(2):
        inv_ref[rows, t * LANES:(t + 1) * LANES] = w[n_a + t] if t <= tile else jnp.zeros((PANEL, LANES), F32)
    if k == R // PANEL - 1:
        return
    first = (k + 1) * PANEL // LANES
    right = split3(jnp.concatenate(w, axis=1))
    left = [s[:, (first - tile) * LANES:n_a * LANES] for s in right]
    order = ((0, 0), (0, 1), (1, 0), (0, 2), (2, 0), (1, 1))
    update = lax.dot_general(jnp.concatenate([left[i] for i, _ in order], axis=0), jnp.concatenate([right[j] for _, j in order], axis=0), (((0,), (0,)), ((), ())), preferred_element_type=F32)
    below = slice(first * LANES, R)
    a_ref[below, tile * LANES:] -= update[:, :n_a * LANES]
    x_ref[below, :(tile + 1) * LANES] -= update[:, n_a * LANES:]


def inverse_kernel(g_ref, after_ref, inv_ref, a_ref, x_ref):
    a_ref[...] = g_ref[...]
    x_ref[...] = (lax.broadcasted_iota(jnp.int32, (R, R), 0) == lax.broadcasted_iota(jnp.int32, (R, R), 1)).astype(F32)
    for k in range(R // PANEL):
        panel_step(k, a_ref, x_ref, inv_ref)


def inverse_factor(gram_matrix, after):
    return pl.pallas_call(
        inverse_kernel,
        out_shape=jax.ShapeDtypeStruct((R, R), F32),
        in_specs=[pl.BlockSpec(memory_space=pltpu.VMEM), pl.BlockSpec(memory_space=pl.ANY)],
        out_specs=pl.BlockSpec(memory_space=pltpu.VMEM),
        scratch_shapes=[pltpu.VMEM((R, R), F32), pltpu.VMEM((R, R), F32)],
        compiler_params=pltpu.CompilerParams(vmem_limit_bytes=24 << 20),
        cost_estimate=pl.CostEstimate(flops=10**8, bytes_accessed=30 * 10**6, transcendentals=0),
    )(gram_matrix, after)


def shards(factor, gradient, sketch_ids):
    rows, cols = factor.shape
    z, y, c, x = (lax.axis_index(a) for a in ALL)
    owner = z // (NZ // NX)
    offset = rows * (((z % (NZ // NX)) * NY + y) * NC + c)
    mine = (x == owner).astype(F32)

    strip = jnp.pad(gradient.T, ((0, 4), (0, 0)))
    plane = lax.all_gather(strip, ("z", "y"), axis=0, tiled=True)

    grad32 = gradient.astype(F32)
    sketch = sketch_ids.astype(F32)
    small = jnp.concatenate([dot(grad32, sketch, 0, 0), decay_rate * dot(factor, sketch, 1, 0)], axis=0)
    small = jnp.sum(spread(small, "x", NX), axis=0)
    inner, decayed = small[:gradient.shape[1]], small[gradient.shape[1]:]
    place = (lax.broadcasted_iota(jnp.int32, (cols, rows), 0) == offset + lax.broadcasted_iota(jnp.int32, (cols, rows), 1)).astype(F32)
    partial = dot(jnp.concatenate([grad32, mine * place], axis=1), jnp.concatenate([inner, decayed], axis=0), 1, 0)
    piece = scatter(scatter_core(partial, c), ("z", "y"), NZ * NY)
    piece = join(spread(piece, ("z", "y"), NZ * NY))
    ranged = lax.all_gather(piece, "c", axis=0, tiled=True)

    here = mine * lax.dynamic_slice_in_dim(ranged, offset, rows, 0)
    gram = dot(lax.dynamic_slice_in_dim(ranged, c * 128, 128, 1), ranged, 0, 0)
    wide = gradient.shape[1]
    part = jnp.concatenate([gram, here, dot(grad32, ranged, 0, 0), decay_rate * dot(factor, ranged, 1, 0)], axis=0)
    part = jnp.sum(spread(part, "x", NX), axis=0)
    gram, own_rows = part[:128], part[128:128 + rows]
    left = part[128:128 + rows + wide]
    gram_matrix = lax.all_gather(gram, "c", axis=0, tiled=True) / B

    right = jnp.concatenate([part[128 + rows + wide:], part[128 + rows:128 + rows + wide]], axis=0)
    core = dot(left, right, 0, 0).reshape(NC, NX, 32, 256)
    core = lax.dynamic_index_in_dim(core, x, 1, keepdims=False).reshape(64, 256)
    core = scatter_core(core, c)
    inverse = inverse_factor(gram_matrix, core)
    core = scatter(core, "y", NY)
    late = (core[0, 0] > 0).astype(jnp.int32) >> 1
    core = jnp.sum(spread(core, "z", NZ), axis=0)

    pair = 2 * rows
    start = offset - rows * c + late
    block = lax.dynamic_slice(plane, (0, start // LANES * LANES), (plane.shape[0], LANES))
    place = (lax.broadcasted_iota(jnp.int32, (LANES, pair), 0) == start % LANES + lax.broadcasted_iota(jnp.int32, (LANES, pair), 1))
    place = (place & (x == owner)).astype(BF16)
    picked = lax.dot_general(place, block, (((0,), (1,)), ((), ())), preferred_element_type=F32).astype(BF16)
    total = picked
    for k in range(1, NX):
        pairs = []
        for d in range(NZ * NY * NC):
            src = (d // (NY * NC)) // (NZ // NX)
            pairs.append((d * NX + src, d * NX + (src + k) % NX))
        total = total + lax.ppermute(picked, ALL, pairs)
    outer_sum = lax.dot_general(total, plane, (((1,), (0,)), ((), ())), preferred_element_type=F32)

    core = join(spread(core, ("x", "y"), NX * NY))
    core = core + 0.0 * outer_sum[:1, :1]
    core = lax.all_gather(core, "c", axis=0, tiled=True)

    range_basis = dot(own_rows, inverse, 1, 1)
    projected_core = dot(dot(inverse, core, 1, 0), inverse, 1, 1) / B
    factor_new = decay_rate * factor + scatter_core(outer_sum, c)
    return (factor_new, range_basis, projected_core)


def solution(mesh):
    fine = Mesh(mesh.devices.reshape(NZ, NY, NC, NX), ALL)
    f = ("z", "y", "c")
    return jax.shard_map(
        shards,
        mesh=fine,
        in_specs=(P(f, "x"), P("x", f), P("x", None)),
        out_specs=(P(f, "x"), P(f, None), P()),
        check_vma=False,
    )
```

```python
import jax
import jax.numpy as jnp
from jax import lax
from jax.experimental import pallas as pl
from jax.experimental.pallas import tpu as pltpu
from jax.sharding import Mesh, PartitionSpec as P

B = 3072
decay_rate = 0.9
NZ, NY, NC, NX = 12, 8, 2, 4
ALL = ("z", "y", "c", "x")
F32 = jnp.float32
BF16 = jnp.bfloat16
R, PANEL, GROUP, LANES = 256, 32, 8, 128
HI = lax.Precision.HIGHEST


def dot(a, b, ca, cb):
    return lax.dot_general(a, b, (((ca,), (cb,)), ((), ())), precision=HI, preferred_element_type=F32)


def spread(v, axis, n):
    return lax.all_to_all(jnp.broadcast_to(v[None], (n,) + v.shape), axis, 0, 0)


def swap_core(v):
    return lax.ppermute(v, "c", [(0, 1), (1, 0)])


def scatter_core(v, core):
    half = v.shape[0] // 2
    mine = lax.dynamic_slice_in_dim(v, core * half, half, 0)
    other = lax.dynamic_slice_in_dim(v, (1 - core) * half, half, 0)
    return mine + swap_core(other)


def scatter(v, axis, n):
    return jnp.sum(lax.all_to_all(v.reshape(n, v.shape[0] // n, v.shape[1]), axis, 0, 0), axis=0)


def after(v, w):
    return v + (0.0 * w[:1, :1]).astype(v.dtype)


def join(v):
    return v.reshape(v.shape[0] * v.shape[1], v.shape[2])


def split3(v):
    high = v.astype(BF16); rest = v - high.astype(F32)
    mid = rest.astype(BF16)
    return high, mid, (rest - mid.astype(F32)).astype(BF16)


def panel_step(k, a_ref, x_ref, inv_ref):
    tile = k * PANEL // LANES
    rows = slice(k * PANEL, (k + 1) * PANEL)
    n_a = 2 - tile
    w = [a_ref[rows, t * LANES:(t + 1) * LANES] for t in range(tile, 2)]
    w += [x_ref[rows, t * LANES:(t + 1) * LANES] for t in range(tile + 1)]
    lane0 = k * PANEL - tile * LANES
    row = lax.broadcasted_iota(jnp.int32, (PANEL, LANES), 0)
    pivots = jnp.ones((PANEL, LANES), F32)
    for g in range(PANEL // GROUP):
        cols = [jnp.broadcast_to(w[0][:, lane0 + g * GROUP + j:lane0 + g * GROUP + j + 1], (PANEL, LANES)) for j in range(GROUP)]
        for j in range(GROUP):
            at = g * GROUP + j
            pivot = cols[j][at:at + 1, :]
            factor = jnp.where(row > at, cols[j] * (1.0 / pivot), 0.0)
            for t in range(j + 1, GROUP):
                cols[t] = cols[t] - factor * cols[t][at:at + 1, :]
            w = [v - factor * v[at:at + 1, :] for v in w]
            pivots = jnp.where(row == at, pivot, pivots)
    scale = lax.rsqrt(pivots)
    w = [v * scale for v in w]
    for t in range(2):
        inv_ref[rows, t * LANES:(t + 1) * LANES] = w[n_a + t] if t <= tile else jnp.zeros((PANEL, LANES), F32)
    if k == R // PANEL - 1:
        return
    first = (k + 1) * PANEL // LANES
    right = split3(jnp.concatenate(w, axis=1))
    left = [s[:, (first - tile) * LANES:n_a * LANES] for s in right]
    order = ((0, 0), (0, 1), (1, 0), (0, 2), (2, 0), (1, 1))
    update = lax.dot_general(jnp.concatenate([left[i] for i, _ in order], axis=0), jnp.concatenate([right[j] for _, j in order], axis=0), (((0,), (0,)), ((), ())), preferred_element_type=F32)
    below = slice(first * LANES, R)
    a_ref[below, tile * LANES:] -= update[:, :n_a * LANES]
    x_ref[below, :(tile + 1) * LANES] -= update[:, n_a * LANES:]


def inverse_kernel(g_ref, after_ref, inv_ref, a_ref, x_ref):
    a_ref[...] = g_ref[...]
    x_ref[...] = (lax.broadcasted_iota(jnp.int32, (R, R), 0) == lax.broadcasted_iota(jnp.int32, (R, R), 1)).astype(F32)
    for k in range(R // PANEL):
        panel_step(k, a_ref, x_ref, inv_ref)


def inverse_factor(gram_matrix, after):
    return pl.pallas_call(
        inverse_kernel,
        out_shape=jax.ShapeDtypeStruct((R, R), F32),
        in_specs=[pl.BlockSpec(memory_space=pltpu.VMEM), pl.BlockSpec(memory_space=pl.ANY)],
        out_specs=pl.BlockSpec(memory_space=pltpu.VMEM),
        scratch_shapes=[pltpu.VMEM((R, R), F32), pltpu.VMEM((R, R), F32)],
        compiler_params=pltpu.CompilerParams(vmem_limit_bytes=24 << 20),
        cost_estimate=pl.CostEstimate(flops=10**8, bytes_accessed=30 * 10**6, transcendentals=0),
    )(gram_matrix, after)


def front_kernel(grad_ref, factor_ref, sketch_ref, small_ref, strip_ref):
    wide, rows = grad_ref.shape[0], factor_ref.shape[0]
    sketch = sketch_ref[...].astype(F32).astype(BF16)
    grad = grad_ref[...]
    strip_ref[...] = jnp.concatenate([grad.astype(F32), jnp.zeros((strip_ref.shape[0] - wide, grad.shape[1]), F32)], axis=0).astype(BF16)
    inner = jnp.dot(grad, sketch, preferred_element_type=F32)
    parts = jnp.dot(jnp.concatenate(split3(factor_ref[...]), axis=0), sketch, preferred_element_type=F32)
    decayed = decay_rate * (parts[:rows] + (parts[rows:2 * rows] + parts[2 * rows:]))
    for k in range(NX):
        small_ref[k, :wide, :] = inner
        small_ref[k, wide:, :] = decayed


def front(grad, factor, sketch_ids):
    wide, rows, cols = grad.shape[0], factor.shape[0], sketch_ids.shape[1]
    whole = pl.BlockSpec(memory_space=pltpu.VMEM)
    return pl.pallas_call(
        front_kernel,
        out_shape=(jax.ShapeDtypeStruct((NX, wide + rows, cols), F32), jax.ShapeDtypeStruct((24, grad.shape[1]), BF16)),
        in_specs=[whole] * 3,
        out_specs=(whole, whole),
        compiler_params=pltpu.CompilerParams(vmem_limit_bytes=24 << 20),
        cost_estimate=pl.CostEstimate(flops=10**8, bytes_accessed=4 * 10**6, transcendentals=0),
    )(grad, factor, sketch_ids)


def shards(factor, gradient, sketch_ids):
    rows, cols = factor.shape
    z, y, c, x = (lax.axis_index(a) for a in ALL)
    owner = z // (NZ // NX)
    offset = rows * (((z % (NZ // NX)) * NY + y) * NC + c)
    mine = (x == owner).astype(F32)

    small, strip = front(gradient.T, factor, sketch_ids)
    plane = lax.all_gather(strip, ("z", "y"), axis=0, tiled=True)
    grad32 = gradient.astype(F32)
    small = jnp.sum(lax.all_to_all(small, "x", 0, 0), axis=0)
    inner, decayed = small[:gradient.shape[1]], small[gradient.shape[1]:]
    place = (lax.broadcasted_iota(jnp.int32, (cols, rows), 0) == offset + lax.broadcasted_iota(jnp.int32, (cols, rows), 1)).astype(F32)
    partial = dot(jnp.concatenate([grad32, mine * place], axis=1), jnp.concatenate([inner, decayed], axis=0), 1, 0)
    piece = scatter(scatter_core(partial, c), ("z", "y"), NZ * NY)
    piece = join(spread(piece, ("z", "y"), NZ * NY))
    ranged = lax.all_gather(piece, "c", axis=0, tiled=True)

    here = mine * lax.dynamic_slice_in_dim(ranged, offset, rows, 0)
    gram = dot(lax.dynamic_slice_in_dim(ranged, c * 128, 128, 1), ranged, 0, 0)
    wide = gradient.shape[1]
    part = jnp.concatenate([gram, here, dot(grad32, ranged, 0, 0), decay_rate * dot(factor, ranged, 1, 0)], axis=0)
    part = jnp.sum(spread(part, "x", NX), axis=0)
    own_rows = part[128:128 + rows]
    left = part[128:128 + rows + wide]
    right = jnp.concatenate([part[128 + rows + wide:], part[128 + rows:128 + rows + wide]], axis=0)
    core = dot(left, right, 0, 0).reshape(NC, NX, 32, 256)
    core = lax.dynamic_index_in_dim(core, x, 1, keepdims=False).reshape(64, 256)
    both = lax.all_gather(jnp.concatenate([part[:128], core], axis=0), "c", axis=0, tiled=False)
    gram_matrix = both[:, :128].reshape(R, R) / B
    core = lax.dynamic_slice_in_dim(both[0, 128:] + both[1, 128:], 32 * c, 32, 0)
    inverse = inverse_factor(gram_matrix, core)
    core = scatter(core, "y", NY)
    late = (core[0, 0] > 0).astype(jnp.int32) >> 1
    core = jnp.sum(spread(core, "z", NZ), axis=0)

    pair = 2 * rows
    start = offset - rows * c + late
    block = lax.dynamic_slice(plane, (0, start // LANES * LANES), (plane.shape[0], LANES))
    place = (lax.broadcasted_iota(jnp.int32, (LANES, pair), 0) == start % LANES + lax.broadcasted_iota(jnp.int32, (LANES, pair), 1))
    place = (place & (x == owner)).astype(BF16)
    picked = lax.dot_general(place, block, (((0,), (1,)), ((), ())), preferred_element_type=F32).astype(BF16)
    total = picked
    for k in range(1, NX):
        pairs = []
        for d in range(NZ * NY * NC):
            src = (d // (NY * NC)) // (NZ // NX)
            pairs.append((d * NX + src, d * NX + (src + k) % NX))
        total = total + lax.ppermute(picked, ALL, pairs)
    outer_sum = lax.dot_general(total, plane, (((1,), (0,)), ((), ())), preferred_element_type=F32)
    factor_new = decay_rate * factor + scatter_core(outer_sum, c)

    core = join(spread(core, ("x", "y"), NX * NY))
    core = after(core, factor_new)
    core = lax.all_gather(core, "c", axis=0, tiled=True)

    range_basis = dot(own_rows, inverse, 1, 1)
    projected_core = dot(dot(inverse, core, 1, 0), inverse, 1, 1) / B
    return (factor_new, range_basis, projected_core)


def solution(mesh):
    fine = Mesh(mesh.devices.reshape(NZ, NY, NC, NX), ALL)
    f = ("z", "y", "c")
    return jax.shard_map(
        shards,
        mesh=fine,
        in_specs=(P(f, "x"), P("x", f), P("x", None)),
        out_specs=(P(f, "x"), P(f, None), P()),
        check_vma=False,
    )
```

```python
import jax
import jax.numpy as jnp
from jax import lax
from jax.experimental import pallas as pl
from jax.experimental.pallas import tpu as pltpu
from jax.sharding import Mesh, PartitionSpec as P

B = 3072
decay_rate = 0.9
NZ, NY, NC, NX = 12, 8, 2, 4
ALL = ("z", "y", "c", "x")
F32 = jnp.float32
BF16 = jnp.bfloat16
R, PANEL, GROUP, LANES = 256, 32, 8, 128
HI = lax.Precision.HIGHEST


def dot(a, b, ca, cb):
    return lax.dot_general(a, b, (((ca,), (cb,)), ((), ())), precision=HI, preferred_element_type=F32)


def spread(v, axis, n):
    return lax.all_to_all(jnp.broadcast_to(v[None], (n,) + v.shape), axis, 0, 0)


def swap_core(v):
    return lax.ppermute(v, "c", [(0, 1), (1, 0)])


def scatter_core(v, core):
    half = v.shape[0] // 2
    mine = lax.dynamic_slice_in_dim(v, core * half, half, 0)
    other = lax.dynamic_slice_in_dim(v, (1 - core) * half, half, 0)
    return mine + swap_core(other)


def scatter(v, axis, n):
    return jnp.sum(lax.all_to_all(v.reshape(n, v.shape[0] // n, v.shape[1]), axis, 0, 0), axis=0)


def nothing(w):
    return (w[0, 0] > 0).astype(jnp.int32) >> 1


def after(v, w):
    return v + nothing(w).astype(v.dtype)


def join(v):
    return v.reshape(v.shape[0] * v.shape[1], v.shape[2])


def split3(v):
    high = v.astype(BF16); rest = v - high.astype(F32)
    mid = rest.astype(BF16)
    return high, mid, (rest - mid.astype(F32)).astype(BF16)


def panel_step(k, a_ref, x_ref, inv_ref):
    tile = k * PANEL // LANES
    rows = slice(k * PANEL, (k + 1) * PANEL)
    n_a = 2 - tile
    w = [a_ref[rows, t * LANES:(t + 1) * LANES] for t in range(tile, 2)]
    w += [x_ref[rows, t * LANES:(t + 1) * LANES] for t in range(tile + 1)]
    lane0 = k * PANEL - tile * LANES
    row = lax.broadcasted_iota(jnp.int32, (PANEL, LANES), 0)
    pivots = jnp.ones((PANEL, LANES), F32)
    for g in range(PANEL // GROUP):
        cols = [jnp.broadcast_to(w[0][:, lane0 + g * GROUP + j:lane0 + g * GROUP + j + 1], (PANEL, LANES)) for j in range(GROUP)]
        for j in range(GROUP):
            at = g * GROUP + j
            pivot = cols[j][at:at + 1, :]
            factor = jnp.where(row > at, cols[j] * (1.0 / pivot), 0.0)
            for t in range(j + 1, GROUP):
                cols[t] = cols[t] - factor * cols[t][at:at + 1, :]
            w = [v - factor * v[at:at + 1, :] for v in w]
            pivots = jnp.where(row == at, pivot, pivots)
    scale = lax.rsqrt(pivots)
    w = [v * scale for v in w]
    for t in range(2):
        inv_ref[rows, t * LANES:(t + 1) * LANES] = w[n_a + t] if t <= tile else jnp.zeros((PANEL, LANES), F32)
    if k == R // PANEL - 1:
        return
    first = (k + 1) * PANEL // LANES
    right = split3(jnp.concatenate(w, axis=1))
    left = [s[:, (first - tile) * LANES:n_a * LANES] for s in right]
    order = ((0, 0), (0, 1), (1, 0), (0, 2), (2, 0), (1, 1))
    update = lax.dot_general(jnp.concatenate([left[i] for i, _ in order], axis=0), jnp.concatenate([right[j] for _, j in order], axis=0), (((0,), (0,)), ((), ())), preferred_element_type=F32)
    below = slice(first * LANES, R)
    a_ref[below, tile * LANES:] -= update[:, :n_a * LANES]
    x_ref[below, :(tile + 1) * LANES] -= update[:, n_a * LANES:]


def inverse_kernel(both_ref, after_ref, inv_ref, a_ref, x_ref):
    for core in range(NC):
        a_ref[64 * core:64 * core + 64, :] = both_ref[core, :64, :] * (1.0 / B)
        for k in range(2):
            at = LANES + 64 * core + 32 * k
            a_ref[at:at + 32, :LANES] = jnp.zeros((32, LANES), F32)
            a_ref[at:at + 32, LANES:] = both_ref[core, 64:96, k * LANES:(k + 1) * LANES] * (1.0 / B)
    x_ref[...] = (lax.broadcasted_iota(jnp.int32, (R, R), 0) == lax.broadcasted_iota(jnp.int32, (R, R), 1)).astype(F32)
    for k in range(R // PANEL):
        panel_step(k, a_ref, x_ref, inv_ref)


def inverse_factor(both, after):
    return pl.pallas_call(
        inverse_kernel,
        out_shape=jax.ShapeDtypeStruct((R, R), F32),
        in_specs=[pl.BlockSpec(memory_space=pltpu.VMEM), pl.BlockSpec(memory_space=pl.ANY)],
        out_specs=pl.BlockSpec(memory_space=pltpu.VMEM),
        scratch_shapes=[pltpu.VMEM((R, R), F32), pltpu.VMEM((R, R), F32)],
        compiler_params=pltpu.CompilerParams(vmem_limit_bytes=24 << 20),
        cost_estimate=pl.CostEstimate(flops=10**8, bytes_accessed=30 * 10**6, transcendentals=0),
    )(both, after)


def front_kernel(grad_hbm, factor_hbm, sketch_hbm, small_ref, strip_ref, grad_ref, factor_ref, sketch_ref, sems):
    pairs = ((grad_hbm, grad_ref), (factor_hbm, factor_ref), (sketch_hbm, sketch_ref))
    copies = [pltpu.make_async_copy(src, dst, sems.at[i]) for i, (src, dst) in enumerate(pairs)]
    for copy in copies:
        copy.start()
    wide, rows = grad_ref.shape[0], factor_ref.shape[0]
    copies[0].wait()
    grad = grad_ref[...]
    strip_ref[...] = jnp.concatenate([grad.astype(F32), jnp.zeros((strip_ref.shape[0] - wide, grad.shape[1]), F32)], axis=0).astype(BF16)
    copies[1].wait()
    pieces = jnp.concatenate(split3(factor_ref[...]), axis=0)
    copies[2].wait()
    sketch = sketch_ref[...].astype(F32).astype(BF16)
    inner = jnp.dot(grad, sketch, preferred_element_type=F32)
    parts = jnp.dot(pieces, sketch, preferred_element_type=F32)
    decayed = decay_rate * (parts[:rows] + (parts[rows:2 * rows] + parts[2 * rows:]))
    for k in range(NX):
        small_ref[k, :wide, :] = inner
        small_ref[k, wide:, :] = decayed


def front(grad, factor, sketch_ids):
    wide, rows, cols = grad.shape[0], factor.shape[0], sketch_ids.shape[1]
    whole = pl.BlockSpec(memory_space=pltpu.VMEM)
    return pl.pallas_call(
        front_kernel,
        out_shape=(jax.ShapeDtypeStruct((NX, wide + rows, cols), F32), jax.ShapeDtypeStruct((24, grad.shape[1]), BF16)),
        in_specs=[pl.BlockSpec(memory_space=pl.ANY)] * 3,
        out_specs=(whole, whole),
        scratch_shapes=[pltpu.VMEM(v.shape, v.dtype) for v in (grad, factor, sketch_ids)] + [pltpu.SemaphoreType.DMA((3,))],
        compiler_params=pltpu.CompilerParams(vmem_limit_bytes=56 << 20),
        cost_estimate=pl.CostEstimate(flops=10**8, bytes_accessed=4 * 10**6, transcendentals=0),
    )(grad, factor, sketch_ids)


def middle_kernel(at_ref, ranged_ref, grad_ref, factor_ref, part_ref):
    offset, mine, core = pl.multiple_of(at_ref[0], 16), at_ref[1], at_ref[2]
    wide, rows = grad_ref.shape[0], factor_ref.shape[0]
    ranged = ranged_ref[...]
    halves = [ranged[:, :LANES], ranged[:, LANES:]]
    moved = [pltpu.roll(v, 64, 1) for v in halves]
    low = lax.broadcasted_iota(jnp.int32, halves[0].shape, 1) < 64
    pick = jnp.where(core == 0, jnp.where(low, halves[0], moved[1]), jnp.where(low, moved[0], halves[1]))
    gram = dot(pick, ranged, 0, 0)
    here = jnp.where(mine == 1, ranged_ref[pl.ds(offset, rows), :], 0.0)
    weighted = sum(jnp.dot(grad_ref[...], v, preferred_element_type=F32) for v in split3(ranged))
    applied = decay_rate * dot(factor_ref[...], ranged, 1, 0)
    for k in range(NX):
        part_ref[k, :64, :] = gram[:64]
        part_ref[k, 64:96, :LANES] = gram[64:96, LANES:]
        part_ref[k, 64:96, LANES:] = gram[96:, LANES:]
        part_ref[k, 96:96 + rows, :] = here
        part_ref[k, 96 + rows:96 + rows + wide, :] = weighted
        part_ref[k, 96 + rows + wide:, :] = applied


def middle(at, ranged, grad, factor):
    whole = pl.BlockSpec(memory_space=pltpu.VMEM)
    return pl.pallas_call(
        middle_kernel,
        out_shape=jax.ShapeDtypeStruct((NX, 96 + 2 * factor.shape[0] + grad.shape[0], R), F32),
        in_specs=[pl.BlockSpec(memory_space=pltpu.SMEM)] + [whole] * 3,
        out_specs=whole,
        compiler_params=pltpu.CompilerParams(vmem_limit_bytes=24 << 20),
        cost_estimate=pl.CostEstimate(flops=10**8, bytes_accessed=4 * 10**6, transcendentals=0),
    )(at, ranged, grad, factor)


def shards(factor, gradient, sketch_ids):
    rows, cols = factor.shape
    z, y, c, x = (lax.axis_index(a) for a in ALL)
    owner = z // (NZ // NX)
    offset = rows * (((z % (NZ // NX)) * NY + y) * NC + c)
    mine = (x == owner).astype(F32)

    small, strip = front(gradient.T, factor, sketch_ids)
    plane = lax.all_gather(strip, ("z", "y"), axis=0, tiled=True)
    grad32 = gradient.astype(F32)
    small = jnp.sum(lax.all_to_all(small, "x", 0, 0), axis=0)
    inner, decayed = small[:gradient.shape[1]], small[gradient.shape[1]:]
    place = (lax.broadcasted_iota(jnp.int32, (cols, rows), 0) == offset + lax.broadcasted_iota(jnp.int32, (cols, rows), 1)).astype(F32)
    partial = dot(jnp.concatenate([grad32, mine * place], axis=1), jnp.concatenate([inner, decayed], axis=0), 1, 0)
    piece = scatter(scatter_core(partial, c), ("z", "y"), NZ * NY)
    piece = join(spread(piece, ("z", "y"), NZ * NY))
    ranged = lax.all_gather(piece, "c", axis=0, tiled=True)

    wide = gradient.shape[1]
    at = jnp.stack([offset, (x == owner).astype(jnp.int32), c])
    part = jnp.sum(lax.all_to_all(middle(at, ranged, gradient.T, factor), "x", 0, 0), axis=0)
    own_rows = part[96:96 + rows]
    left = part[96:96 + rows + wide]
    right = jnp.concatenate([part[96 + rows + wide:], part[96 + rows:96 + rows + wide]], axis=0)
    core = dot(left, right, 0, 0).reshape(NC, NX, 32, 256)
    core = lax.dynamic_index_in_dim(core, x, 1, keepdims=False).reshape(64, 256)
    both = lax.all_gather(jnp.concatenate([part[:96], core], axis=0), "c", axis=0, tiled=False)
    core = lax.dynamic_slice_in_dim(both[0, 96:] + both[1, 96:], 32 * c, 32, 0)
    inverse = inverse_factor(both, core)
    core = core_y = scatter(core, "y", NY)
    range_basis = dot(own_rows, inverse, 1, 1)
    core = jnp.sum(spread(core, "z", NZ), axis=0)

    pair = 2 * rows
    start = offset - rows * c + nothing(core_y)
    block = lax.dynamic_slice(plane, (0, start // LANES * LANES), (plane.shape[0], LANES))
    place = (lax.broadcasted_iota(jnp.int32, (LANES, pair), 0) == start % LANES + lax.broadcasted_iota(jnp.int32, (LANES, pair), 1))
    place = (place & (x == owner)).astype(BF16)
    picked = lax.dot_general(place, block, (((0,), (1,)), ((), ())), preferred_element_type=F32).astype(BF16)
    total = picked
    for k in range(1, NX):
        pairs = []
        for d in range(NZ * NY * NC):
            src = (d // (NY * NC)) // (NZ // NX)
            pairs.append((d * NX + src, d * NX + (src + k) % NX))
        total = total + lax.ppermute(picked, ALL, pairs)
    outer_sum = lax.dot_general(total, plane, (((1,), (0,)), ((), ())), preferred_element_type=F32)
    factor_new = decay_rate * factor + scatter_core(outer_sum, c)

    core = join(spread(core, ("x", "y"), NX * NY))
    core = after(core, outer_sum)
    core = lax.all_gather(core, "c", axis=0, tiled=True)

    projected_core = dot(dot(inverse, core, 1, 0), inverse, 1, 1) / B
    return (factor_new, range_basis, projected_core)


def solution(mesh):
    fine = Mesh(mesh.devices.reshape(NZ, NY, NC, NX), ALL)
    f = ("z", "y", "c")
    return jax.shard_map(
        shards,
        mesh=fine,
        in_specs=(P(f, "x"), P("x", f), P("x", None)),
        out_specs=(P(f, "x"), P(f, None), P()),
        check_vma=False,
    )
```

```python
import jax
import jax.numpy as jnp
from jax import lax
from jax.experimental import pallas as pl
from jax.experimental.pallas import tpu as pltpu
from jax.sharding import Mesh, PartitionSpec as P

B = 3072
decay_rate = 0.9
NZ, NY, NC, NX = 12, 8, 2, 4
ALL = ("z", "y", "c", "x")
F32 = jnp.float32
BF16 = jnp.bfloat16
R, PANEL, GROUP, LANES = 256, 32, 8, 128
HI = lax.Precision.HIGHEST


def dot(a, b, ca, cb):
    return lax.dot_general(a, b, (((ca,), (cb,)), ((), ())), precision=HI, preferred_element_type=F32)


def spread(v, axis, n):
    return lax.all_to_all(jnp.broadcast_to(v[None], (n,) + v.shape), axis, 0, 0)


def swap_core(v):
    return lax.ppermute(v, "c", [(0, 1), (1, 0)])


def scatter_core(v, core):
    half = v.shape[0] // 2
    mine = lax.dynamic_slice_in_dim(v, core * half, half, 0)
    other = lax.dynamic_slice_in_dim(v, (1 - core) * half, half, 0)
    return mine + swap_core(other)


def scatter(v, axis, n):
    return jnp.sum(lax.all_to_all(v.reshape(n, v.shape[0] // n, v.shape[1]), axis, 0, 0), axis=0)


def nothing(w):
    return (w[0, 0] > 0).astype(jnp.int32) >> 1


def after(v, w):
    return v + nothing(w).astype(v.dtype)


def join(v):
    return v.reshape(v.shape[0] * v.shape[1], v.shape[2])


def split3(v):
    high = v.astype(BF16); rest = v - high.astype(F32)
    mid = rest.astype(BF16)
    return high, mid, (rest - mid.astype(F32)).astype(BF16)


def panel_step(k, a_ref, x_ref, inv_ref):
    tile = k * PANEL // LANES
    rows = slice(k * PANEL, (k + 1) * PANEL)
    n_a = 2 - tile
    w = [a_ref[rows, t * LANES:(t + 1) * LANES] for t in range(tile, 2)]
    w += [x_ref[rows, t * LANES:(t + 1) * LANES] for t in range(tile + 1)]
    lane0 = k * PANEL - tile * LANES
    row = lax.broadcasted_iota(jnp.int32, (PANEL, LANES), 0)
    pivots = jnp.ones((PANEL, LANES), F32)
    for g in range(PANEL // GROUP):
        cols = [jnp.broadcast_to(w[0][:, lane0 + g * GROUP + j:lane0 + g * GROUP + j + 1], (PANEL, LANES)) for j in range(GROUP)]
        for j in range(GROUP):
            at = g * GROUP + j
            pivot = cols[j][at:at + 1, :]
            factor = jnp.where(row > at, cols[j] * (1.0 / pivot), 0.0)
            for t in range(j + 1, GROUP):
                cols[t] = cols[t] - factor * cols[t][at:at + 1, :]
            w = [v - factor * v[at:at + 1, :] for v in w]
            pivots = jnp.where(row == at, pivot, pivots)
    scale = lax.rsqrt(pivots)
    w = [v * scale for v in w]
    for t in range(2):
        inv_ref[rows, t * LANES:(t + 1) * LANES] = w[n_a + t] if t <= tile else jnp.zeros((PANEL, LANES), F32)
    if k == R // PANEL - 1:
        return
    first = (k + 1) * PANEL // LANES
    right = split3(jnp.concatenate(w, axis=1))
    left = [s[:, (first - tile) * LANES:n_a * LANES] for s in right]
    order = ((0, 0), (0, 1), (1, 0), (0, 2), (2, 0), (1, 1))
    update = lax.dot_general(jnp.concatenate([left[i] for i, _ in order], axis=0), jnp.concatenate([right[j] for _, j in order], axis=0), (((0,), (0,)), ((), ())), preferred_element_type=F32)
    below = slice(first * LANES, R)
    a_ref[below, tile * LANES:] -= update[:, :n_a * LANES]
    x_ref[below, :(tile + 1) * LANES] -= update[:, n_a * LANES:]


def inverse_kernel(both_ref, after_ref, inv_ref, a_ref, x_ref):
    for core in range(NC):
        a_ref[64 * core:64 * core + 64, :] = both_ref[core, :64, :] * (1.0 / B)
        for k in range(2):
            at = LANES + 64 * core + 32 * k
            a_ref[at:at + 32, :LANES] = jnp.zeros((32, LANES), F32)
            a_ref[at:at + 32, LANES:] = both_ref[core, 64:96, k * LANES:(k + 1) * LANES] * (1.0 / B)
    x_ref[...] = (lax.broadcasted_iota(jnp.int32, (R, R), 0) == lax.broadcasted_iota(jnp.int32, (R, R), 1)).astype(F32)
    for k in range(R // PANEL):
        panel_step(k, a_ref, x_ref, inv_ref)


def inverse_factor(both, after):
    return pl.pallas_call(
        inverse_kernel,
        out_shape=jax.ShapeDtypeStruct((R, R), F32),
        in_specs=[pl.BlockSpec(memory_space=pltpu.VMEM), pl.BlockSpec(memory_space=pl.ANY)],
        out_specs=pl.BlockSpec(memory_space=pltpu.VMEM),
        scratch_shapes=[pltpu.VMEM((R, R), F32), pltpu.VMEM((R, R), F32)],
        compiler_params=pltpu.CompilerParams(vmem_limit_bytes=24 << 20),
        cost_estimate=pl.CostEstimate(flops=10**8, bytes_accessed=30 * 10**6, transcendentals=0),
    )(both, after)


def front_kernel(grad_hbm, factor_hbm, sketch_hbm, small_ref, strip_ref, grad_ref, factor_ref, sketch_ref, sems):
    pairs = ((grad_hbm, grad_ref), (factor_hbm, factor_ref), (sketch_hbm, sketch_ref))
    copies = [pltpu.make_async_copy(src, dst, sems.at[i]) for i, (src, dst) in enumerate(pairs)]
    for copy in copies:
        copy.start()
    wide, rows = grad_ref.shape[0], factor_ref.shape[0]
    copies[0].wait()
    grad = grad_ref[...]
    strip_ref[...] = jnp.concatenate([grad.astype(F32), jnp.zeros((strip_ref.shape[0] - wide, grad.shape[1]), F32)], axis=0).astype(BF16)
    copies[1].wait()
    pieces = jnp.concatenate(split3(factor_ref[...]), axis=0)
    copies[2].wait()
    sketch = sketch_ref[...].astype(F32).astype(BF16)
    inner = jnp.dot(grad, sketch, preferred_element_type=F32)
    parts = jnp.dot(pieces, sketch, preferred_element_type=F32)
    decayed = decay_rate * (parts[:rows] + (parts[rows:2 * rows] + parts[2 * rows:]))
    for k in range(NX):
        small_ref[k, :wide, :] = inner
        small_ref[k, wide:, :] = decayed


def front(grad, factor, sketch_ids):
    wide, rows, cols = grad.shape[0], factor.shape[0], sketch_ids.shape[1]
    whole = pl.BlockSpec(memory_space=pltpu.VMEM)
    return pl.pallas_call(
        front_kernel,
        out_shape=(jax.ShapeDtypeStruct((NX, wide + rows, cols), F32), jax.ShapeDtypeStruct((24, grad.shape[1]), BF16)),
        in_specs=[pl.BlockSpec(memory_space=pl.ANY)] * 3,
        out_specs=(whole, whole),
        scratch_shapes=[pltpu.VMEM(v.shape, v.dtype) for v in (grad, factor, sketch_ids)] + [pltpu.SemaphoreType.DMA((3,))],
        compiler_params=pltpu.CompilerParams(vmem_limit_bytes=56 << 20),
        cost_estimate=pl.CostEstimate(flops=10**8, bytes_accessed=4 * 10**6, transcendentals=0),
    )(grad, factor, sketch_ids)


def middle_kernel(at_ref, ranged_ref, grad_ref, factor_ref, part_ref):
    offset, mine, core = pl.multiple_of(at_ref[0], 16), at_ref[1], at_ref[2]
    wide, rows = grad_ref.shape[0], factor_ref.shape[0]
    ranged = ranged_ref[...]
    halves = [ranged[:, :LANES], ranged[:, LANES:]]
    moved = [pltpu.roll(v, 64, 1) for v in halves]
    low = lax.broadcasted_iota(jnp.int32, halves[0].shape, 1) < 64
    pick = jnp.where(core == 0, jnp.where(low, halves[0], moved[1]), jnp.where(low, moved[0], halves[1]))
    gram = dot(pick, ranged, 0, 0)
    here = jnp.where(mine == 1, ranged_ref[pl.ds(offset, rows), :], 0.0)
    weighted = sum(jnp.dot(grad_ref[...], v, preferred_element_type=F32) for v in split3(ranged))
    applied = decay_rate * dot(factor_ref[...], ranged, 1, 0)
    for k in range(NX):
        part_ref[k, :64, :] = gram[:64]
        part_ref[k, 64:96, :LANES] = gram[64:96, LANES:]
        part_ref[k, 64:96, LANES:] = gram[96:, LANES:]
        part_ref[k, 96:96 + rows, :] = here
        part_ref[k, 96 + rows:96 + rows + wide, :] = weighted
        part_ref[k, 96 + rows + wide:, :] = applied


def middle(at, ranged, grad, factor):
    whole = pl.BlockSpec(memory_space=pltpu.VMEM)
    return pl.pallas_call(
        middle_kernel,
        out_shape=jax.ShapeDtypeStruct((NX, 96 + 2 * factor.shape[0] + grad.shape[0], R), F32),
        in_specs=[pl.BlockSpec(memory_space=pltpu.SMEM)] + [whole] * 3,
        out_specs=whole,
        compiler_params=pltpu.CompilerParams(vmem_limit_bytes=24 << 20),
        cost_estimate=pl.CostEstimate(flops=10**8, bytes_accessed=4 * 10**6, transcendentals=0),
    )(at, ranged, grad, factor)


def shards(factor, gradient, sketch_ids):
    rows, cols = factor.shape
    z, y, c, x = (lax.axis_index(a) for a in ALL)
    owner = z // (NZ // NX)
    offset = rows * (((z % (NZ // NX)) * NY + y) * NC + c)
    mine = (x == owner).astype(F32)

    small, strip = front(gradient.T, factor, sketch_ids)
    plane = lax.all_gather(strip, ("z", "y"), axis=0, tiled=True)
    grad32 = gradient.astype(F32)
    small = jnp.sum(lax.all_to_all(small, "x", 0, 0), axis=0)
    inner, decayed = small[:gradient.shape[1]], small[gradient.shape[1]:]
    place = (lax.broadcasted_iota(jnp.int32, (cols, rows), 0) == offset + lax.broadcasted_iota(jnp.int32, (cols, rows), 1)).astype(F32)
    partial = dot(jnp.concatenate([grad32, mine * place], axis=1), jnp.concatenate([inner, decayed], axis=0), 1, 0)
    piece = scatter(scatter_core(partial, c), ("z", "y"), NZ * NY)
    piece = join(spread(piece, ("z", "y"), NZ * NY))
    ranged = lax.all_gather(piece, "c", axis=0, tiled=True)

    wide = gradient.shape[1]
    at = jnp.stack([offset, (x == owner).astype(jnp.int32), c])
    part = jnp.sum(lax.all_to_all(middle(at, ranged, gradient.T, factor), "x", 0, 0), axis=0)
    own_rows = part[96:96 + rows]
    left = part[96:96 + rows + wide]
    right = jnp.concatenate([part[96 + rows + wide:], part[96 + rows:96 + rows + wide]], axis=0)
    core = dot(left, right, 0, 0).reshape(NC, NX, 32, 256)
    core = lax.dynamic_index_in_dim(core, x, 1, keepdims=False).reshape(64, 256)
    both = lax.all_gather(jnp.concatenate([part[:96], core], axis=0), "c", axis=0, tiled=False)
    core = lax.dynamic_slice_in_dim(both[0, 96:] + both[1, 96:], 32 * c, 32, 0)
    inverse = inverse_factor(both, core)
    core = core_y = scatter(core, "y", NY)
    range_basis = dot(own_rows, inverse, 1, 1)
    core = jnp.sum(spread(core, "z", NZ), axis=0)

    pair = 2 * rows
    start = offset - rows * c + nothing(core)
    block = lax.dynamic_slice(plane, (0, start // LANES * LANES), (plane.shape[0], LANES))
    place = (lax.broadcasted_iota(jnp.int32, (LANES, pair), 0) == start % LANES + lax.broadcasted_iota(jnp.int32, (LANES, pair), 1))
    place = (place & (x == owner)).astype(BF16)
    picked = lax.dot_general(place, block, (((0,), (1,)), ((), ())), preferred_element_type=F32).astype(BF16)
    total = picked
    for k in range(1, NX):
        pairs = []
        for d in range(NZ * NY * NC):
            src = (d // (NY * NC)) // (NZ // NX)
            pairs.append((d * NX + src, d * NX + (src + k) % NX))
        total = total + lax.ppermute(picked, ALL, pairs)
    outer_sum = lax.dot_general(total, plane, (((1,), (0,)), ((), ())), preferred_element_type=F32)
    factor_new = decay_rate * factor + scatter_core(outer_sum, c)

    core = join(spread(core, ("x", "y"), NX * NY))
    core = after(core, picked)
    core = lax.all_gather(core, "c", axis=0, tiled=True)

    projected_core = dot(dot(inverse, core, 1, 0), inverse, 1, 1) / B
    return (factor_new, range_basis, projected_core)


def solution(mesh):
    fine = Mesh(mesh.devices.reshape(NZ, NY, NC, NX), ALL)
    f = ("z", "y", "c")
    return jax.shard_map(
        shards,
        mesh=fine,
        in_specs=(P(f, "x"), P("x", f), P("x", None)),
        out_specs=(P(f, "x"), P(f, None), P()),
        check_vma=False,
    )
```

```python
import jax
import jax.numpy as jnp
from jax import lax
from jax.experimental import pallas as pl
from jax.experimental.pallas import tpu as pltpu
from jax.sharding import Mesh, PartitionSpec as P

B = 3072
decay_rate = 0.9
NZ, NY, NC, NX = 12, 8, 2, 4
ALL = ("z", "y", "c", "x")
F32 = jnp.float32
BF16 = jnp.bfloat16
R, PANEL, GROUP, LANES = 256, 32, 8, 128
HI = lax.Precision.HIGHEST


def dot(a, b, ca, cb):
    return lax.dot_general(a, b, (((ca,), (cb,)), ((), ())), precision=HI, preferred_element_type=F32)


def spread(v, axis, n):
    return lax.all_to_all(jnp.broadcast_to(v[None], (n,) + v.shape), axis, 0, 0)


def swap_core(v):
    return lax.ppermute(v, "c", [(0, 1), (1, 0)])


def scatter_core(v, core):
    half = v.shape[0] // 2
    mine = lax.dynamic_slice_in_dim(v, core * half, half, 0)
    other = lax.dynamic_slice_in_dim(v, (1 - core) * half, half, 0)
    return mine + swap_core(other)


def scatter(v, axis, n):
    return jnp.sum(lax.all_to_all(v.reshape(n, v.shape[0] // n, v.shape[1]), axis, 0, 0), axis=0)


def nothing(w):
    return (w[0, 0] > 0).astype(jnp.int32) >> 1


def after(v, w):
    return v + nothing(w).astype(v.dtype)


def join(v):
    return v.reshape(v.shape[0] * v.shape[1], v.shape[2])


def split3(v):
    high = v.astype(BF16); rest = v - high.astype(F32)
    mid = rest.astype(BF16)
    return high, mid, (rest - mid.astype(F32)).astype(BF16)


def panel_step(k, a_ref, x_ref, inv_ref):
    tile = k * PANEL // LANES
    rows = slice(k * PANEL, (k + 1) * PANEL)
    n_a = 2 - tile
    w = [a_ref[rows, t * LANES:(t + 1) * LANES] for t in range(tile, 2)]
    w += [x_ref[rows, t * LANES:(t + 1) * LANES] for t in range(tile + 1)]
    lane0 = k * PANEL - tile * LANES
    row = lax.broadcasted_iota(jnp.int32, (PANEL, LANES), 0)
    pivots = jnp.ones((PANEL, LANES), F32)
    for g in range(PANEL // GROUP):
        cols = [jnp.broadcast_to(w[0][:, lane0 + g * GROUP + j:lane0 + g * GROUP + j + 1], (PANEL, LANES)) for j in range(GROUP)]
        for j in range(GROUP):
            at = g * GROUP + j
            pivot = cols[j][at:at + 1, :]
            factor = jnp.where(row > at, cols[j] * (1.0 / pivot), 0.0)
            for t in range(j + 1, GROUP):
                cols[t] = cols[t] - factor * cols[t][at:at + 1, :]
            w = [v - factor * v[at:at + 1, :] for v in w]
            pivots = jnp.where(row == at, pivot, pivots)
    scale = lax.rsqrt(pivots)
    w = [v * scale for v in w]
    for t in range(2):
        inv_ref[rows, t * LANES:(t + 1) * LANES] = w[n_a + t] if t <= tile else jnp.zeros((PANEL, LANES), F32)
    if k == R // PANEL - 1:
        return
    first = (k + 1) * PANEL // LANES
    right = split3(jnp.concatenate(w, axis=1))
    left = [s[:, (first - tile) * LANES:n_a * LANES] for s in right]
    order = ((0, 0), (0, 1), (1, 0), (0, 2), (2, 0), (1, 1))
    update = lax.dot_general(jnp.concatenate([left[i] for i, _ in order], axis=0), jnp.concatenate([right[j] for _, j in order], axis=0), (((0,), (0,)), ((), ())), preferred_element_type=F32)
    below = slice(first * LANES, R)
    a_ref[below, tile * LANES:] -= update[:, :n_a * LANES]
    x_ref[below, :(tile + 1) * LANES] -= update[:, n_a * LANES:]


def inverse_kernel(both_ref, after_ref, inv_ref, a_ref, x_ref):
    for core in range(NC):
        a_ref[64 * core:64 * core + 64, :] = both_ref[core, :64, :] * (1.0 / B)
        for k in range(2):
            at = LANES + 64 * core + 32 * k
            a_ref[at:at + 32, :LANES] = jnp.zeros((32, LANES), F32)
            a_ref[at:at + 32, LANES:] = both_ref[core, 64:96, k * LANES:(k + 1) * LANES] * (1.0 / B)
    x_ref[...] = (lax.broadcasted_iota(jnp.int32, (R, R), 0) == lax.broadcasted_iota(jnp.int32, (R, R), 1)).astype(F32)
    for k in range(R // PANEL):
        panel_step(k, a_ref, x_ref, inv_ref)


def inverse_factor(both, after):
    return pl.pallas_call(
        inverse_kernel,
        out_shape=jax.ShapeDtypeStruct((R, R), F32),
        in_specs=[pl.BlockSpec(memory_space=pltpu.VMEM), pl.BlockSpec(memory_space=pl.ANY)],
        out_specs=pl.BlockSpec(memory_space=pltpu.VMEM),
        scratch_shapes=[pltpu.VMEM((R, R), F32), pltpu.VMEM((R, R), F32)],
        compiler_params=pltpu.CompilerParams(vmem_limit_bytes=24 << 20),
        cost_estimate=pl.CostEstimate(flops=10**8, bytes_accessed=30 * 10**6, transcendentals=0),
    )(both, after)


def front_kernel(grad_hbm, factor_hbm, sketch_hbm, small_ref, strip_ref, grad_ref, factor_ref, sketch_ref, sems):
    pairs = ((grad_hbm, grad_ref), (factor_hbm, factor_ref), (sketch_hbm, sketch_ref))
    copies = [pltpu.make_async_copy(src, dst, sems.at[i]) for i, (src, dst) in enumerate(pairs)]
    for copy in copies:
        copy.start()
    wide, rows = grad_ref.shape[0], factor_ref.shape[0]
    copies[0].wait()
    grad = grad_ref[...]
    strip_ref[...] = jnp.concatenate([grad.astype(F32), jnp.zeros((strip_ref.shape[0] - wide, grad.shape[1]), F32)], axis=0).astype(BF16)
    copies[1].wait()
    pieces = jnp.concatenate(split3(factor_ref[...]), axis=0)
    copies[2].wait()
    sketch = sketch_ref[...].astype(F32).astype(BF16)
    inner = jnp.dot(grad, sketch, preferred_element_type=F32)
    parts = jnp.dot(pieces, sketch, preferred_element_type=F32)
    decayed = decay_rate * (parts[:rows] + (parts[rows:2 * rows] + parts[2 * rows:]))
    for k in range(NX):
        small_ref[k, :wide, :] = inner
        small_ref[k, wide:, :] = decayed


def front(grad, factor, sketch_ids):
    wide, rows, cols = grad.shape[0], factor.shape[0], sketch_ids.shape[1]
    whole = pl.BlockSpec(memory_space=pltpu.VMEM)
    return pl.pallas_call(
        front_kernel,
        out_shape=(jax.ShapeDtypeStruct((NX, wide + rows, cols), F32), jax.ShapeDtypeStruct((24, grad.shape[1]), BF16)),
        in_specs=[pl.BlockSpec(memory_space=pl.ANY)] * 3,
        out_specs=(whole, whole),
        scratch_shapes=[pltpu.VMEM(v.shape, v.dtype) for v in (grad, factor, sketch_ids)] + [pltpu.SemaphoreType.DMA((3,))],
        compiler_params=pltpu.CompilerParams(vmem_limit_bytes=56 << 20),
        cost_estimate=pl.CostEstimate(flops=10**8, bytes_accessed=4 * 10**6, transcendentals=0),
    )(grad, factor, sketch_ids)


def middle_kernel(at_ref, ranged_ref, grad_ref, factor_ref, part_ref):
    offset, mine, core = pl.multiple_of(at_ref[0], 16), at_ref[1], at_ref[2]
    wide, rows = grad_ref.shape[0], factor_ref.shape[0]
    ranged = ranged_ref[...]
    halves = [ranged[:, :LANES], ranged[:, LANES:]]
    moved = [pltpu.roll(v, 64, 1) for v in halves]
    low = lax.broadcasted_iota(jnp.int32, halves[0].shape, 1) < 64
    pick = jnp.where(core == 0, jnp.where(low, halves[0], moved[1]), jnp.where(low, moved[0], halves[1]))
    gram = dot(pick, ranged, 0, 0)
    here = jnp.where(mine == 1, ranged_ref[pl.ds(offset, rows), :], 0.0)
    weighted = sum(jnp.dot(grad_ref[...], v, preferred_element_type=F32) for v in split3(ranged))
    applied = decay_rate * dot(factor_ref[...], ranged, 1, 0)
    for k in range(NX):
        part_ref[k, :64, :] = gram[:64]
        part_ref[k, 64:96, :LANES] = gram[64:96, LANES:]
        part_ref[k, 64:96, LANES:] = gram[96:, LANES:]
        part_ref[k, 96:96 + rows, :] = here
        part_ref[k, 96 + rows:96 + rows + wide, :] = weighted
        part_ref[k, 96 + rows + wide:, :] = applied


def middle(at, ranged, grad, factor):
    whole = pl.BlockSpec(memory_space=pltpu.VMEM)
    return pl.pallas_call(
        middle_kernel,
        out_shape=jax.ShapeDtypeStruct((NX, 96 + 2 * factor.shape[0] + grad.shape[0], R), F32),
        in_specs=[pl.BlockSpec(memory_space=pltpu.SMEM)] + [whole] * 3,
        out_specs=whole,
        compiler_params=pltpu.CompilerParams(vmem_limit_bytes=24 << 20),
        cost_estimate=pl.CostEstimate(flops=10**8, bytes_accessed=4 * 10**6, transcendentals=0),
    )(at, ranged, grad, factor)


def shards(factor, gradient, sketch_ids):
    rows, cols = factor.shape
    z, y, c, x = (lax.axis_index(a) for a in ALL)
    owner = z // (NZ // NX)
    offset = rows * (((z % (NZ // NX)) * NY + y) * NC + c)
    mine = (x == owner).astype(F32)

    small, strip = front(gradient.T, factor, sketch_ids)
    grad32 = gradient.astype(F32)
    small = jnp.sum(lax.all_to_all(small, "x", 0, 0), axis=0)
    inner, decayed = small[:gradient.shape[1]], small[gradient.shape[1]:]
    place = (lax.broadcasted_iota(jnp.int32, (cols, rows), 0) == offset + lax.broadcasted_iota(jnp.int32, (cols, rows), 1)).astype(F32)
    partial = dot(jnp.concatenate([grad32, mine * place], axis=1), jnp.concatenate([inner, decayed], axis=0), 1, 0)
    partial = scatter_core(partial, c)
    strip = after(strip, partial)
    strips = [strip]
    for k in range(1, NY):
        strips.append(lax.ppermute(strip, "y", [(d, (d + k) % NY) for d in range(NY)]))
    piece = scatter(partial, ("z", "y"), NZ * NY)
    plane = lax.all_gather(after(jnp.concatenate(strips, axis=0), piece), "z", axis=0, tiled=True)
    piece = join(spread(piece, ("z", "y"), NZ * NY))
    ranged = lax.all_gather(piece, "c", axis=0, tiled=True)

    wide = gradient.shape[1]
    at = jnp.stack([offset, (x == owner).astype(jnp.int32), c])
    part = jnp.sum(lax.all_to_all(middle(at, ranged, gradient.T, factor), "x", 0, 0), axis=0)
    own_rows = part[96:96 + rows]
    left = part[96:96 + rows + wide]
    right = jnp.concatenate([part[96 + rows + wide:], part[96 + rows:96 + rows + wide]], axis=0)
    core = dot(left, right, 0, 0).reshape(NC, NX, 32, 256)
    core = lax.dynamic_index_in_dim(core, x, 1, keepdims=False).reshape(64, 256)
    both = lax.all_gather(jnp.concatenate([part[:96], core], axis=0), "c", axis=0, tiled=False)
    core = lax.dynamic_slice_in_dim(both[0, 96:] + both[1, 96:], 32 * c, 32, 0)
    inverse = inverse_factor(both, core)
    core = core_y = scatter(core, "y", NY)
    range_basis = dot(own_rows, inverse, 1, 1)
    core = jnp.sum(spread(core, "z", NZ), axis=0)

    pair = 2 * rows
    start = offset - rows * c + nothing(core_y)
    block = lax.dynamic_slice(plane, (0, start // LANES * LANES), (plane.shape[0], LANES))
    place = (lax.broadcasted_iota(jnp.int32, (LANES, pair), 0) == start % LANES + lax.broadcasted_iota(jnp.int32, (LANES, pair), 1))
    place = (place & (x == owner)).astype(BF16)
    picked = lax.dot_general(place, block, (((0,), (1,)), ((), ())), preferred_element_type=F32).astype(BF16)
    total = picked
    for k in range(1, NX):
        pairs = []
        for d in range(NZ * NY * NC):
            src = (d // (NY * NC)) // (NZ // NX)
            pairs.append((d * NX + src, d * NX + (src + k) % NX))
        total = total + lax.ppermute(picked, ALL, pairs)
    outer_sum = lax.dot_general(total, plane, (((1,), (0,)), ((), ())), preferred_element_type=F32)
    factor_new = decay_rate * factor + scatter_core(outer_sum, c)

    core = join(spread(core, ("x", "y"), NX * NY))
    core = after(core, outer_sum)
    core = lax.all_gather(core, "c", axis=0, tiled=True)

    projected_core = dot(dot(inverse, core, 1, 0), inverse, 1, 1) / B
    return (factor_new, range_basis, projected_core)


def solution(mesh):
    fine = Mesh(mesh.devices.reshape(NZ, NY, NC, NX), ALL)
    f = ("z", "y", "c")
    return jax.shard_map(
        shards,
        mesh=fine,
        in_specs=(P(f, "x"), P("x", f), P("x", None)),
        out_specs=(P(f, "x"), P(f, None), P()),
        check_vma=False,
    )
```

```python
import jax
import jax.numpy as jnp
from jax import lax
from jax.experimental import pallas as pl
from jax.experimental.pallas import tpu as pltpu
from jax.sharding import Mesh, PartitionSpec as P

B = 3072
decay_rate = 0.9
NZ, NY, NC, NX = 12, 8, 2, 4
ALL = ("z", "y", "c", "x")
F32 = jnp.float32
BF16 = jnp.bfloat16
R, PANEL, GROUP, LANES = 256, 32, 8, 128
HI = lax.Precision.HIGHEST


def dot(a, b, ca, cb):
    return lax.dot_general(a, b, (((ca,), (cb,)), ((), ())), precision=HI, preferred_element_type=F32)


def spread(v, axis, n):
    return lax.all_to_all(jnp.broadcast_to(v[None], (n,) + v.shape), axis, 0, 0)


def swap_core(v):
    return lax.ppermute(v, "c", [(0, 1), (1, 0)])


def scatter_core(v, core):
    half = v.shape[0] // 2
    mine = lax.dynamic_slice_in_dim(v, core * half, half, 0)
    other = lax.dynamic_slice_in_dim(v, (1 - core) * half, half, 0)
    return mine + swap_core(other)


def scatter(v, axis, n):
    return jnp.sum(lax.all_to_all(v.reshape(n, v.shape[0] // n, v.shape[1]), axis, 0, 0), axis=0)


def nothing(w):
    return (w[0, 0] > 0).astype(jnp.int32) >> 1


def after(v, w):
    return v + nothing(w).astype(v.dtype)


def join(v):
    return v.reshape(v.shape[0] * v.shape[1], v.shape[2])


def split3(v):
    high = v.astype(BF16); rest = v - high.astype(F32)
    mid = rest.astype(BF16)
    return high, mid, (rest - mid.astype(F32)).astype(BF16)


def panel_step(k, a_ref, x_ref, inv_ref):
    tile = k * PANEL // LANES
    rows = slice(k * PANEL, (k + 1) * PANEL)
    n_a = 2 - tile
    w = [a_ref[rows, t * LANES:(t + 1) * LANES] for t in range(tile, 2)]
    w += [x_ref[rows, t * LANES:(t + 1) * LANES] for t in range(tile + 1)]
    lane0 = k * PANEL - tile * LANES
    row = lax.broadcasted_iota(jnp.int32, (PANEL, LANES), 0)
    pivots = jnp.ones((PANEL, LANES), F32)
    for g in range(PANEL // GROUP):
        cols = [jnp.broadcast_to(w[0][:, lane0 + g * GROUP + j:lane0 + g * GROUP + j + 1], (PANEL, LANES)) for j in range(GROUP)]
        for j in range(GROUP):
            at = g * GROUP + j
            pivot = cols[j][at:at + 1, :]
            factor = jnp.where(row > at, cols[j] * (1.0 / pivot), 0.0)
            for t in range(j + 1, GROUP):
                cols[t] = cols[t] - factor * cols[t][at:at + 1, :]
            w = [v - factor * v[at:at + 1, :] for v in w]
            pivots = jnp.where(row == at, pivot, pivots)
    scale = lax.rsqrt(pivots)
    w = [v * scale for v in w]
    for t in range(2):
        inv_ref[rows, t * LANES:(t + 1) * LANES] = w[n_a + t] if t <= tile else jnp.zeros((PANEL, LANES), F32)
    if k == R // PANEL - 1:
        return
    first = (k + 1) * PANEL // LANES
    right = split3(jnp.concatenate(w, axis=1))
    left = [s[:, (first - tile) * LANES:n_a * LANES] for s in right]
    order = ((0, 0), (0, 1), (1, 0), (0, 2), (2, 0), (1, 1))
    update = lax.dot_general(jnp.concatenate([left[i] for i, _ in order], axis=0), jnp.concatenate([right[j] for _, j in order], axis=0), (((0,), (0,)), ((), ())), preferred_element_type=F32)
    below = slice(first * LANES, R)
    a_ref[below, tile * LANES:] -= update[:, :n_a * LANES]
    x_ref[below, :(tile + 1) * LANES] -= update[:, n_a * LANES:]


def inverse_kernel(both_ref, after_ref, inv_ref, a_ref, x_ref):
    for core in range(NC):
        a_ref[64 * core:64 * core + 64, :] = both_ref[core, :64, :] * (1.0 / B)
        for k in range(2):
            at = LANES + 64 * core + 32 * k
            a_ref[at:at + 32, :LANES] = jnp.zeros((32, LANES), F32)
            a_ref[at:at + 32, LANES:] = both_ref[core, 64:96, k * LANES:(k + 1) * LANES] * (1.0 / B)
    x_ref[...] = (lax.broadcasted_iota(jnp.int32, (R, R), 0) == lax.broadcasted_iota(jnp.int32, (R, R), 1)).astype(F32)
    for k in range(R // PANEL):
        panel_step(k, a_ref, x_ref, inv_ref)


def inverse_factor(both, after):
    return pl.pallas_call(
        inverse_kernel,
        out_shape=jax.ShapeDtypeStruct((R, R), F32),
        in_specs=[pl.BlockSpec(memory_space=pltpu.VMEM), pl.BlockSpec(memory_space=pl.ANY)],
        out_specs=pl.BlockSpec(memory_space=pltpu.VMEM),
        scratch_shapes=[pltpu.VMEM((R, R), F32), pltpu.VMEM((R, R), F32)],
        compiler_params=pltpu.CompilerParams(vmem_limit_bytes=24 << 20),
        cost_estimate=pl.CostEstimate(flops=10**8, bytes_accessed=30 * 10**6, transcendentals=0),
    )(both, after)


def strip_kernel(grad_hbm, strip_ref, grad_ref, sem):
    copy = pltpu.make_async_copy(grad_hbm, grad_ref, sem)
    copy.start()
    copy.wait()
    grad = grad_ref[...].astype(F32)
    strip_ref[...] = jnp.concatenate([grad, jnp.zeros((strip_ref.shape[0] - grad.shape[0], grad.shape[1]), F32)], axis=0).astype(BF16)


def padded(grad):
    return pl.pallas_call(
        strip_kernel,
        out_shape=jax.ShapeDtypeStruct((24, grad.shape[1]), BF16),
        in_specs=[pl.BlockSpec(memory_space=pl.ANY)],
        out_specs=pl.BlockSpec(memory_space=pltpu.VMEM),
        scratch_shapes=[pltpu.VMEM(grad.shape, BF16), pltpu.SemaphoreType.DMA],
        compiler_params=pltpu.CompilerParams(vmem_limit_bytes=56 << 20),
        cost_estimate=pl.CostEstimate(flops=10**5, bytes_accessed=10**5, transcendentals=0),
    )(grad)


def front_kernel(grad_hbm, factor_hbm, sketch_hbm, small_ref, grad_ref, factor_ref, sketch_ref, sems):
    pairs = ((grad_hbm, grad_ref), (factor_hbm, factor_ref), (sketch_hbm, sketch_ref))
    copies = [pltpu.make_async_copy(src, dst, sems.at[i]) for i, (src, dst) in enumerate(pairs)]
    for copy in copies:
        copy.start()
    wide, rows = grad_ref.shape[0], factor_ref.shape[0]
    copies[0].wait()
    grad = grad_ref[...]
    copies[1].wait()
    pieces = jnp.concatenate(split3(factor_ref[...]), axis=0)
    copies[2].wait()
    sketch = sketch_ref[...].astype(F32).astype(BF16)
    inner = jnp.dot(grad, sketch, preferred_element_type=F32)
    parts = jnp.dot(pieces, sketch, preferred_element_type=F32)
    decayed = decay_rate * (parts[:rows] + (parts[rows:2 * rows] + parts[2 * rows:]))
    for k in range(NX):
        small_ref[k, :wide, :] = inner
        small_ref[k, wide:, :] = decayed


def front(grad, factor, sketch_ids):
    wide, rows, cols = grad.shape[0], factor.shape[0], sketch_ids.shape[1]
    whole = pl.BlockSpec(memory_space=pltpu.VMEM)
    return pl.pallas_call(
        front_kernel,
        out_shape=jax.ShapeDtypeStruct((NX, wide + rows, cols), F32),
        in_specs=[pl.BlockSpec(memory_space=pl.ANY)] * 3,
        out_specs=whole,
        scratch_shapes=[pltpu.VMEM(v.shape, v.dtype) for v in (grad, factor, sketch_ids)] + [pltpu.SemaphoreType.DMA((3,))],
        compiler_params=pltpu.CompilerParams(vmem_limit_bytes=56 << 20),
        cost_estimate=pl.CostEstimate(flops=10**8, bytes_accessed=4 * 10**6, transcendentals=0),
    )(grad, factor, sketch_ids)


def middle_kernel(at_ref, ranged_ref, grad_ref, factor_ref, part_ref):
    offset, mine, core = pl.multiple_of(at_ref[0], 16), at_ref[1], at_ref[2]
    wide, rows = grad_ref.shape[0], factor_ref.shape[0]
    ranged = ranged_ref[...]
    halves = [ranged[:, :LANES], ranged[:, LANES:]]
    moved = [pltpu.roll(v, 64, 1) for v in halves]
    low = lax.broadcasted_iota(jnp.int32, halves[0].shape, 1) < 64
    pick = jnp.where(core == 0, jnp.where(low, halves[0], moved[1]), jnp.where(low, moved[0], halves[1]))
    gram = dot(pick, ranged, 0, 0)
    here = jnp.where(mine == 1, ranged_ref[pl.ds(offset, rows), :], 0.0)
    weighted = sum(jnp.dot(grad_ref[...], v, preferred_element_type=F32) for v in split3(ranged))
    applied = decay_rate * dot(factor_ref[...], ranged, 1, 0)
    for k in range(NX):
        part_ref[k, :64, :] = gram[:64]
        part_ref[k, 64:96, :LANES] = gram[64:96, LANES:]
        part_ref[k, 64:96, LANES:] = gram[96:, LANES:]
        part_ref[k, 96:96 + rows, :] = here
        part_ref[k, 96 + rows:96 + rows + wide, :] = weighted
        part_ref[k, 96 + rows + wide:, :] = applied


def middle(at, ranged, grad, factor):
    whole = pl.BlockSpec(memory_space=pltpu.VMEM)
    return pl.pallas_call(
        middle_kernel,
        out_shape=jax.ShapeDtypeStruct((NX, 96 + 2 * factor.shape[0] + grad.shape[0], R), F32),
        in_specs=[pl.BlockSpec(memory_space=pltpu.SMEM)] + [whole] * 3,
        out_specs=whole,
        compiler_params=pltpu.CompilerParams(vmem_limit_bytes=24 << 20),
        cost_estimate=pl.CostEstimate(flops=10**8, bytes_accessed=4 * 10**6, transcendentals=0),
    )(at, ranged, grad, factor)


def pick_kernel(at_ref, plane_hbm, after_ref, out_ref, block_ref, sem):
    start, mine = at_ref[0], at_ref[1]
    tile = pl.multiple_of((start >> 7) << 7, LANES)
    copy = pltpu.make_async_copy(plane_hbm.at[:, pl.ds(tile, LANES)], block_ref, sem)
    copy.start()
    shape = (out_ref.shape[0], LANES)
    place = lax.broadcasted_iota(jnp.int32, shape, 1) == (start & 127) + lax.broadcasted_iota(jnp.int32, shape, 0)
    place = jnp.where(place, mine.astype(F32), 0.0).astype(BF16)
    copy.wait()
    out_ref[...] = lax.dot_general(place, block_ref[...], (((1,), (1,)), ((), ())), preferred_element_type=F32).astype(BF16)


def pick(at, plane, after, count):
    return pl.pallas_call(
        pick_kernel,
        out_shape=jax.ShapeDtypeStruct((count, plane.shape[0]), BF16),
        in_specs=[pl.BlockSpec(memory_space=pltpu.SMEM)] + [pl.BlockSpec(memory_space=pl.ANY)] * 2,
        out_specs=pl.BlockSpec(memory_space=pltpu.VMEM),
        scratch_shapes=[pltpu.VMEM((plane.shape[0], LANES), BF16), pltpu.SemaphoreType.DMA],
        compiler_params=pltpu.CompilerParams(vmem_limit_bytes=56 << 20),
        cost_estimate=pl.CostEstimate(flops=10**8, bytes_accessed=30 * 10**6, transcendentals=0),
    )(at, plane, after)


def shards(factor, gradient, sketch_ids):
    rows, cols = factor.shape
    z, y, c, x = (lax.axis_index(a) for a in ALL)
    owner = z // (NZ // NX)
    offset = rows * (((z % (NZ // NX)) * NY + y) * NC + c)
    mine = (x == owner).astype(F32)

    strip = padded(gradient.T)
    small = front(gradient.T, factor, sketch_ids)
    plane = lax.all_gather(strip, ("z", "y"), axis=0, tiled=True)
    grad32 = gradient.astype(F32)
    small = jnp.sum(lax.all_to_all(small, "x", 0, 0), axis=0)
    inner, decayed = small[:gradient.shape[1]], small[gradient.shape[1]:]
    place = (lax.broadcasted_iota(jnp.int32, (cols, rows), 0) == offset + lax.broadcasted_iota(jnp.int32, (cols, rows), 1)).astype(F32)
    partial = dot(jnp.concatenate([grad32, mine * place], axis=1), jnp.concatenate([inner, decayed], axis=0), 1, 0)
    piece = scatter(scatter_core(partial, c), ("z", "y"), NZ * NY)
    piece = join(spread(piece, ("z", "y"), NZ * NY))
    ranged = lax.all_gather(piece, "c", axis=0, tiled=True)

    wide = gradient.shape[1]
    at = jnp.stack([offset, (x == owner).astype(jnp.int32), c])
    part = jnp.sum(lax.all_to_all(middle(at, ranged, gradient.T, factor), "x", 0, 0), axis=0)
    own_rows = part[96:96 + rows]
    left = part[96:96 + rows + wide]
    right = jnp.concatenate([part[96 + rows + wide:], part[96 + rows:96 + rows + wide]], axis=0)
    core = dot(left, right, 0, 0).reshape(NC, NX, 32, 256)
    core = lax.dynamic_index_in_dim(core, x, 1, keepdims=False).reshape(64, 256)
    both = lax.all_gather(jnp.concatenate([part[:96], core], axis=0), "c", axis=0, tiled=False)
    core = lax.dynamic_slice_in_dim(both[0, 96:] + both[1, 96:], 32 * c, 32, 0)
    inverse = inverse_factor(both, core)
    core = core_y = scatter(core, "y", NY)
    range_basis = dot(own_rows, inverse, 1, 1)

    pair = 2 * rows
    picked = pick(jnp.stack([offset - rows * c, (x == owner).astype(jnp.int32)]), plane, core_y, pair)
    total = picked
    for k in range(1, NX):
        pairs = []
        for d in range(NZ * NY * NC):
            src = (d // (NY * NC)) // (NZ // NX)
            pairs.append((d * NX + src, d * NX + (src + k) % NX))
        total = total + lax.ppermute(picked, ALL, pairs)
    core = after(jnp.sum(spread(core, "z", NZ), axis=0), total)
    outer_sum = lax.dot_general(total, plane, (((1,), (0,)), ((), ())), preferred_element_type=F32)

    core = join(spread(core, ("x", "y"), NX * NY))
    other = lax.dynamic_slice_in_dim(outer_sum, (1 - c) * rows, rows, 0)
    both = lax.all_gather(jnp.concatenate([core] + [other[:, k:k + R] for k in range(0, cols, R)], axis=0), "c", axis=0, tiled=False)
    core = both[:, :128].reshape(R, R)
    other = lax.dynamic_index_in_dim(both[:, 128:], 1 - c, 0, keepdims=False)
    other = jnp.concatenate([other[k:k + rows] for k in range(0, other.shape[0], rows)], axis=1)
    factor_new = decay_rate * factor + (lax.dynamic_slice_in_dim(outer_sum, c * rows, rows, 0) + other)

    projected_core = dot(dot(inverse, core, 1, 0), inverse, 1, 1) / B
    return (factor_new, range_basis, projected_core)


def solution(mesh):
    fine = Mesh(mesh.devices.reshape(NZ, NY, NC, NX), ALL)
    f = ("z", "y", "c")
    return jax.shard_map(
        shards,
        mesh=fine,
        in_specs=(P(f, "x"), P("x", f), P("x", None)),
        out_specs=(P(f, "x"), P(f, None), P()),
        check_vma=False,
    )
```

```python
import jax
import jax.numpy as jnp
from jax import lax
from jax.experimental import pallas as pl
from jax.experimental.pallas import tpu as pltpu
from jax.sharding import Mesh, PartitionSpec as P

B = 3072
decay_rate = 0.9
NZ, NY, NC, NX = 12, 8, 2, 4
ALL = ("z", "y", "c", "x")
F32 = jnp.float32
BF16 = jnp.bfloat16
R, PANEL, GROUP, LANES = 256, 32, 8, 128
HI = lax.Precision.HIGHEST


def dot(a, b, ca, cb):
    return lax.dot_general(a, b, (((ca,), (cb,)), ((), ())), precision=HI, preferred_element_type=F32)


def spread(v, axis, n):
    return lax.all_to_all(jnp.broadcast_to(v[None], (n,) + v.shape), axis, 0, 0)


def swap_core(v):
    return lax.ppermute(v, "c", [(0, 1), (1, 0)])


def scatter_core(v, core):
    half = v.shape[0] // 2
    mine = lax.dynamic_slice_in_dim(v, core * half, half, 0)
    other = lax.dynamic_slice_in_dim(v, (1 - core) * half, half, 0)
    return mine + swap_core(other)


def scatter(v, axis, n):
    return jnp.sum(lax.all_to_all(v.reshape(n, v.shape[0] // n, v.shape[1]), axis, 0, 0), axis=0)


def nothing(w):
    return (w[0, 0] > 0).astype(jnp.int32) >> 1


def after(v, w):
    return v + nothing(w).astype(v.dtype)


def join(v):
    return v.reshape(v.shape[0] * v.shape[1], v.shape[2])


def split3(v):
    high = v.astype(BF16); rest = v - high.astype(F32)
    mid = rest.astype(BF16)
    return high, mid, (rest - mid.astype(F32)).astype(BF16)


def panel_step(k, a_ref, x_ref, inv_ref):
    tile = k * PANEL // LANES
    rows = slice(k * PANEL, (k + 1) * PANEL)
    n_a = 2 - tile
    w = [a_ref[rows, t * LANES:(t + 1) * LANES] for t in range(tile, 2)]
    w += [x_ref[rows, t * LANES:(t + 1) * LANES] for t in range(tile + 1)]
    lane0 = k * PANEL - tile * LANES
    row = lax.broadcasted_iota(jnp.int32, (PANEL, LANES), 0)
    pivots = jnp.ones((PANEL, LANES), F32)
    for g in range(PANEL // GROUP):
        cols = [jnp.broadcast_to(w[0][:, lane0 + g * GROUP + j:lane0 + g * GROUP + j + 1], (PANEL, LANES)) for j in range(GROUP)]
        for j in range(GROUP):
            at = g * GROUP + j
            pivot = cols[j][at:at + 1, :]
            factor = jnp.where(row > at, cols[j] * (1.0 / pivot), 0.0)
            for t in range(j + 1, GROUP):
                cols[t] = cols[t] - factor * cols[t][at:at + 1, :]
            w = [v - factor * v[at:at + 1, :] for v in w]
            pivots = jnp.where(row == at, pivot, pivots)
    scale = lax.rsqrt(pivots)
    w = [v * scale for v in w]
    for t in range(2):
        inv_ref[rows, t * LANES:(t + 1) * LANES] = w[n_a + t] if t <= tile else jnp.zeros((PANEL, LANES), F32)
    if k == R // PANEL - 1:
        return
    first = (k + 1) * PANEL // LANES
    right = split3(jnp.concatenate(w, axis=1))
    left = [s[:, (first - tile) * LANES:n_a * LANES] for s in right]
    order = ((0, 0), (0, 1), (1, 0), (0, 2), (2, 0), (1, 1))
    update = lax.dot_general(jnp.concatenate([left[i] for i, _ in order], axis=0), jnp.concatenate([right[j] for _, j in order], axis=0), (((0,), (0,)), ((), ())), preferred_element_type=F32)
    below = slice(first * LANES, R)
    a_ref[below, tile * LANES:] -= update[:, :n_a * LANES]
    x_ref[below, :(tile + 1) * LANES] -= update[:, n_a * LANES:]


def inverse_kernel(both_ref, after_ref, inv_ref, a_ref, x_ref):
    for core in range(NC):
        a_ref[64 * core:64 * core + 64, :] = both_ref[core, :64, :] * (1.0 / B)
        for k in range(2):
            at = LANES + 64 * core + 32 * k
            a_ref[at:at + 32, :LANES] = jnp.zeros((32, LANES), F32)
            a_ref[at:at + 32, LANES:] = both_ref[core, 64:96, k * LANES:(k + 1) * LANES] * (1.0 / B)
    x_ref[...] = (lax.broadcasted_iota(jnp.int32, (R, R), 0) == lax.broadcasted_iota(jnp.int32, (R, R), 1)).astype(F32)
    for k in range(R // PANEL):
        panel_step(k, a_ref, x_ref, inv_ref)


def inverse_factor(both, after):
    return pl.pallas_call(
        inverse_kernel,
        out_shape=jax.ShapeDtypeStruct((R, R), F32),
        in_specs=[pl.BlockSpec(memory_space=pltpu.VMEM), pl.BlockSpec(memory_space=pl.ANY)],
        out_specs=pl.BlockSpec(memory_space=pltpu.VMEM),
        scratch_shapes=[pltpu.VMEM((R, R), F32), pltpu.VMEM((R, R), F32)],
        compiler_params=pltpu.CompilerParams(vmem_limit_bytes=24 << 20),
        cost_estimate=pl.CostEstimate(flops=10**8, bytes_accessed=30 * 10**6, transcendentals=0),
    )(both, after)


def front_kernel(grad_hbm, factor_hbm, sketch_hbm, small_ref, strip_ref, grad_ref, factor_ref, sketch_ref, sems):
    pairs = ((grad_hbm, grad_ref), (factor_hbm, factor_ref), (sketch_hbm, sketch_ref))
    copies = [pltpu.make_async_copy(src, dst, sems.at[i]) for i, (src, dst) in enumerate(pairs)]
    for copy in copies:
        copy.start()
    wide, rows = grad_ref.shape[0], factor_ref.shape[0]
    copies[0].wait()
    grad = grad_ref[...]
    strip_ref[...] = jnp.concatenate([grad.astype(F32), jnp.zeros((strip_ref.shape[0] - wide, grad.shape[1]), F32)], axis=0).astype(BF16)
    copies[1].wait()
    pieces = jnp.concatenate(split3(factor_ref[...]), axis=0)
    copies[2].wait()
    sketch = sketch_ref[...].astype(F32).astype(BF16)
    inner = jnp.dot(grad, sketch, preferred_element_type=F32)
    parts = jnp.dot(pieces, sketch, preferred_element_type=F32)
    decayed = decay_rate * (parts[:rows] + (parts[rows:2 * rows] + parts[2 * rows:]))
    for k in range(NX):
        small_ref[k, :wide, :] = inner
        small_ref[k, wide:, :] = decayed


def front(grad, factor, sketch_ids):
    wide, rows, cols = grad.shape[0], factor.shape[0], sketch_ids.shape[1]
    whole = pl.BlockSpec(memory_space=pltpu.VMEM)
    return pl.pallas_call(
        front_kernel,
        out_shape=(jax.ShapeDtypeStruct((NX, wide + rows, cols), F32), jax.ShapeDtypeStruct((24, grad.shape[1]), BF16)),
        in_specs=[pl.BlockSpec(memory_space=pl.ANY)] * 3,
        out_specs=(whole, whole),
        scratch_shapes=[pltpu.VMEM(v.shape, v.dtype) for v in (grad, factor, sketch_ids)] + [pltpu.SemaphoreType.DMA((3,))],
        compiler_params=pltpu.CompilerParams(vmem_limit_bytes=56 << 20),
        cost_estimate=pl.CostEstimate(flops=10**8, bytes_accessed=4 * 10**6, transcendentals=0),
    )(grad, factor, sketch_ids)


def middle_kernel(at_ref, ranged_ref, grad_ref, factor_ref, part_ref):
    offset, mine, core = pl.multiple_of(at_ref[0], 16), at_ref[1], at_ref[2]
    wide, rows = grad_ref.shape[0], factor_ref.shape[0]
    ranged = ranged_ref[...]
    halves = [ranged[:, :LANES], ranged[:, LANES:]]
    moved = [pltpu.roll(v, 64, 1) for v in halves]
    low = lax.broadcasted_iota(jnp.int32, halves[0].shape, 1) < 64
    pick = jnp.where(core == 0, jnp.where(low, halves[0], moved[1]), jnp.where(low, moved[0], halves[1]))
    gram = dot(pick, ranged, 0, 0)
    here = jnp.where(mine == 1, ranged_ref[pl.ds(offset, rows), :], 0.0)
    weighted = sum(jnp.dot(grad_ref[...], v, preferred_element_type=F32) for v in split3(ranged))
    applied = decay_rate * dot(factor_ref[...], ranged, 1, 0)
    for k in range(NX):
        part_ref[k, :64, :] = gram[:64]
        part_ref[k, 64:96, :LANES] = gram[64:96, LANES:]
        part_ref[k, 64:96, LANES:] = gram[96:, LANES:]
        part_ref[k, 96:96 + rows, :] = here
        part_ref[k, 96 + rows:96 + rows + wide, :] = weighted
        part_ref[k, 96 + rows + wide:, :] = applied


def middle(at, ranged, grad, factor):
    whole = pl.BlockSpec(memory_space=pltpu.VMEM)
    return pl.pallas_call(
        middle_kernel,
        out_shape=jax.ShapeDtypeStruct((NX, 96 + 2 * factor.shape[0] + grad.shape[0], R), F32),
        in_specs=[pl.BlockSpec(memory_space=pltpu.SMEM)] + [whole] * 3,
        out_specs=whole,
        compiler_params=pltpu.CompilerParams(vmem_limit_bytes=24 << 20),
        cost_estimate=pl.CostEstimate(flops=10**8, bytes_accessed=4 * 10**6, transcendentals=0),
    )(at, ranged, grad, factor)


def pick_kernel(at_ref, plane_hbm, after_ref, out_ref, block_ref, sem):
    start, mine = at_ref[0], at_ref[1]
    tile = pl.multiple_of((start >> 7) << 7, LANES)
    copy = pltpu.make_async_copy(plane_hbm.at[:, pl.ds(tile, LANES)], block_ref, sem)
    copy.start()
    shape = (out_ref.shape[0], LANES)
    place = lax.broadcasted_iota(jnp.int32, shape, 1) == (start & 127) + lax.broadcasted_iota(jnp.int32, shape, 0)
    place = jnp.where(place, mine.astype(F32), 0.0).astype(BF16)
    copy.wait()
    out_ref[...] = lax.dot_general(place, block_ref[...], (((1,), (1,)), ((), ())), preferred_element_type=F32).astype(BF16)


def pick(at, plane, after, count):
    return pl.pallas_call(
        pick_kernel,
        out_shape=jax.ShapeDtypeStruct((count, plane.shape[0]), BF16),
        in_specs=[pl.BlockSpec(memory_space=pltpu.SMEM)] + [pl.BlockSpec(memory_space=pl.ANY)] * 2,
        out_specs=pl.BlockSpec(memory_space=pltpu.VMEM),
        scratch_shapes=[pltpu.VMEM((plane.shape[0], LANES), BF16), pltpu.SemaphoreType.DMA],
        compiler_params=pltpu.CompilerParams(vmem_limit_bytes=56 << 20),
        cost_estimate=pl.CostEstimate(flops=10**8, bytes_accessed=30 * 10**6, transcendentals=0),
    )(at, plane, after)


def shards(factor, gradient, sketch_ids):
    rows, cols = factor.shape
    z, y, c, x = (lax.axis_index(a) for a in ALL)
    owner = z // (NZ // NX)
    offset = rows * (((z % (NZ // NX)) * NY + y) * NC + c)
    mine = (x == owner).astype(F32)

    small, strip = front(gradient.T, factor, sketch_ids)
    plane = lax.all_gather(strip, ("z", "y"), axis=0, tiled=True)
    grad32 = gradient.astype(F32)
    small = jnp.sum(lax.all_to_all(small, "x", 0, 0), axis=0)
    inner, decayed = small[:gradient.shape[1]], small[gradient.shape[1]:]
    place = (lax.broadcasted_iota(jnp.int32, (cols, rows), 0) == offset + lax.broadcasted_iota(jnp.int32, (cols, rows), 1)).astype(F32)
    partial = dot(jnp.concatenate([grad32, mine * place], axis=1), jnp.concatenate([inner, decayed], axis=0), 1, 0)
    piece = scatter(scatter_core(partial, c), ("z", "y"), NZ * NY)
    piece = join(spread(piece, ("z", "y"), NZ * NY))
    ranged = lax.all_gather(piece, "c", axis=0, tiled=True)

    wide = gradient.shape[1]
    at = jnp.stack([offset, (x == owner).astype(jnp.int32), c])
    part = jnp.sum(lax.all_to_all(middle(at, ranged, gradient.T, factor), "x", 0, 0), axis=0)
    own_rows = part[96:96 + rows]
    left = part[96:96 + rows + wide]
    right = jnp.concatenate([part[96 + rows + wide:], part[96 + rows:96 + rows + wide]], axis=0)
    core = dot(left, right, 0, 0).reshape(NC, NX, 32, 256)
    core = lax.dynamic_index_in_dim(core, x, 1, keepdims=False).reshape(64, 256)
    both = lax.all_gather(jnp.concatenate([part[:96], core], axis=0), "c", axis=0, tiled=False)
    core = lax.dynamic_slice_in_dim(both[0, 96:] + both[1, 96:], 32 * c, 32, 0)
    inverse = inverse_factor(both, core)
    core = core_y = scatter(core, "y", NY)
    range_basis = dot(own_rows, inverse, 1, 1)
    core = after(jnp.sum(spread(core, "z", NZ), axis=0), range_basis)

    pair = 2 * rows
    picked = pick(jnp.stack([offset - rows * c, (x == owner).astype(jnp.int32)]), plane, core_y, pair)
    total = picked
    for k in range(1, NX):
        pairs = []
        for d in range(NZ * NY * NC):
            src = (d // (NY * NC)) // (NZ // NX)
            pairs.append((d * NX + src, d * NX + (src + k) % NX))
        total = total + lax.ppermute(picked, ALL, pairs)
    outer_sum = lax.dot_general(total, plane, (((1,), (0,)), ((), ())), preferred_element_type=F32)

    core = join(spread(core, ("x", "y"), NX * NY))
    other = lax.dynamic_slice_in_dim(outer_sum, (1 - c) * rows, rows, 0)
    both = lax.all_gather(jnp.concatenate([core] + [other[:, k:k + R] for k in range(0, cols, R)], axis=0), "c", axis=0, tiled=False)
    core = both[:, :128].reshape(R, R)
    other = lax.dynamic_index_in_dim(both[:, 128:], 1 - c, 0, keepdims=False)
    other = jnp.concatenate([other[k:k + rows] for k in range(0, other.shape[0], rows)], axis=1)
    factor_new = decay_rate * factor + (lax.dynamic_slice_in_dim(outer_sum, c * rows, rows, 0) + other)

    projected_core = dot(dot(inverse, core, 1, 0), inverse, 1, 1) / B
    return (factor_new, range_basis, projected_core)


def solution(mesh):
    fine = Mesh(mesh.devices.reshape(NZ, NY, NC, NX), ALL)
    f = ("z", "y", "c")
    return jax.shard_map(
        shards,
        mesh=fine,
        in_specs=(P(f, "x"), P("x", f), P("x", None)),
        out_specs=(P(f, "x"), P(f, None), P()),
        check_vma=False,
    )
```

```python
import jax
import jax.numpy as jnp
from jax import lax
from jax.experimental import pallas as pl
from jax.experimental.pallas import tpu as pltpu
from jax.sharding import Mesh, PartitionSpec as P

B = 3072
decay_rate = 0.9
NZ, NY, NC, NX = 12, 8, 2, 4
ALL = ("z", "y", "c", "x")
F32 = jnp.float32
BF16 = jnp.bfloat16
R, PANEL, GROUP, LANES = 256, 32, 8, 128
HI = lax.Precision.HIGHEST


def dot(a, b, ca, cb):
    return lax.dot_general(a, b, (((ca,), (cb,)), ((), ())), precision=HI, preferred_element_type=F32)


def spread(v, axis, n):
    return lax.all_to_all(jnp.broadcast_to(v[None], (n,) + v.shape), axis, 0, 0)


def swap_core(v):
    return lax.ppermute(v, "c", [(0, 1), (1, 0)])


def scatter_core(v, core):
    half = v.shape[0] // 2
    mine = lax.dynamic_slice_in_dim(v, core * half, half, 0)
    other = lax.dynamic_slice_in_dim(v, (1 - core) * half, half, 0)
    return mine + swap_core(other)


def scatter(v, axis, n):
    return jnp.sum(lax.all_to_all(v.reshape(n, v.shape[0] // n, v.shape[1]), axis, 0, 0), axis=0)


def nothing(w):
    return (w[0, 0] > 0).astype(jnp.int32) >> 1


def after(v, w):
    return v + nothing(w).astype(v.dtype)


def join(v):
    return v.reshape(v.shape[0] * v.shape[1], v.shape[2])


def split3(v):
    high = v.astype(BF16); rest = v - high.astype(F32)
    mid = rest.astype(BF16)
    return high, mid, (rest - mid.astype(F32)).astype(BF16)


def panel_step(k, a_ref, x_ref, inv_ref):
    tile = k * PANEL // LANES
    rows = slice(k * PANEL, (k + 1) * PANEL)
    n_a = 2 - tile
    w = [a_ref[rows, t * LANES:(t + 1) * LANES] for t in range(tile, 2)]
    w += [x_ref[rows, t * LANES:(t + 1) * LANES] for t in range(tile + 1)]
    lane0 = k * PANEL - tile * LANES
    row = lax.broadcasted_iota(jnp.int32, (PANEL, LANES), 0)
    pivots = jnp.ones((PANEL, LANES), F32)
    for g in range(PANEL // GROUP):
        cols = [jnp.broadcast_to(w[0][:, lane0 + g * GROUP + j:lane0 + g * GROUP + j + 1], (PANEL, LANES)) for j in range(GROUP)]
        for j in range(GROUP):
            at = g * GROUP + j
            pivot = cols[j][at:at + 1, :]
            factor = jnp.where(row > at, cols[j] * (1.0 / pivot), 0.0)
            for t in range(j + 1, GROUP):
                cols[t] = cols[t] - factor * cols[t][at:at + 1, :]
            w = [v - factor * v[at:at + 1, :] for v in w]
            pivots = jnp.where(row == at, pivot, pivots)
    scale = lax.rsqrt(pivots)
    w = [v * scale for v in w]
    for t in range(2):
        inv_ref[rows, t * LANES:(t + 1) * LANES] = w[n_a + t] if t <= tile else jnp.zeros((PANEL, LANES), F32)
    if k == R // PANEL - 1:
        return
    first = (k + 1) * PANEL // LANES
    right = split3(jnp.concatenate(w, axis=1))
    left = [s[:, (first - tile) * LANES:n_a * LANES] for s in right]
    order = ((0, 0), (0, 1), (1, 0), (0, 2), (2, 0), (1, 1))
    update = lax.dot_general(jnp.concatenate([left[i] for i, _ in order], axis=0), jnp.concatenate([right[j] for _, j in order], axis=0), (((0,), (0,)), ((), ())), preferred_element_type=F32)
    below = slice(first * LANES, R)
    a_ref[below, tile * LANES:] -= update[:, :n_a * LANES]
    x_ref[below, :(tile + 1) * LANES] -= update[:, n_a * LANES:]


def inverse_kernel(both_ref, after_ref, inv_ref, a_ref, x_ref):
    for core in range(NC):
        a_ref[64 * core:64 * core + 64, :] = both_ref[core, :64, :] * (1.0 / B)
        for k in range(2):
            at = LANES + 64 * core + 32 * k
            a_ref[at:at + 32, :LANES] = jnp.zeros((32, LANES), F32)
            a_ref[at:at + 32, LANES:] = both_ref[core, 64:96, k * LANES:(k + 1) * LANES] * (1.0 / B)
    x_ref[...] = (lax.broadcasted_iota(jnp.int32, (R, R), 0) == lax.broadcasted_iota(jnp.int32, (R, R), 1)).astype(F32)
    for k in range(R // PANEL):
        panel_step(k, a_ref, x_ref, inv_ref)


def inverse_factor(both, after):
    return pl.pallas_call(
        inverse_kernel,
        out_shape=jax.ShapeDtypeStruct((R, R), F32),
        in_specs=[pl.BlockSpec(memory_space=pltpu.VMEM), pl.BlockSpec(memory_space=pl.ANY)],
        out_specs=pl.BlockSpec(memory_space=pltpu.VMEM),
        scratch_shapes=[pltpu.VMEM((R, R), F32), pltpu.VMEM((R, R), F32)],
        compiler_params=pltpu.CompilerParams(vmem_limit_bytes=24 << 20),
        cost_estimate=pl.CostEstimate(flops=10**8, bytes_accessed=30 * 10**6, transcendentals=0),
    )(both, after)


def front_kernel(grad_hbm, factor_hbm, sketch_hbm, small_ref, strip_ref, grad_ref, factor_ref, sketch_ref, sems):
    pairs = ((grad_hbm, grad_ref), (factor_hbm, factor_ref), (sketch_hbm, sketch_ref))
    copies = [pltpu.make_async_copy(src, dst, sems.at[i]) for i, (src, dst) in enumerate(pairs)]
    for copy in copies:
        copy.start()
    wide, rows = grad_ref.shape[0], factor_ref.shape[0]
    copies[0].wait()
    grad = grad_ref[...]
    strip_ref[...] = jnp.concatenate([grad.astype(F32), jnp.zeros((strip_ref.shape[0] - wide, grad.shape[1]), F32)], axis=0).astype(BF16)
    copies[1].wait()
    pieces = jnp.concatenate(split3(factor_ref[...]), axis=0)
    copies[2].wait()
    sketch = sketch_ref[...].astype(F32).astype(BF16)
    inner = jnp.dot(grad, sketch, preferred_element_type=F32)
    parts = jnp.dot(pieces, sketch, preferred_element_type=F32)
    decayed = decay_rate * (parts[:rows] + (parts[rows:2 * rows] + parts[2 * rows:]))
    for k in range(NX):
        small_ref[k, :wide, :] = inner
        small_ref[k, wide:, :] = decayed


def front(grad, factor, sketch_ids):
    wide, rows, cols = grad.shape[0], factor.shape[0], sketch_ids.shape[1]
    whole = pl.BlockSpec(memory_space=pltpu.VMEM)
    return pl.pallas_call(
        front_kernel,
        out_shape=(jax.ShapeDtypeStruct((NX, wide + rows, cols), F32), jax.ShapeDtypeStruct((24, grad.shape[1]), BF16)),
        in_specs=[pl.BlockSpec(memory_space=pl.ANY)] * 3,
        out_specs=(whole, whole),
        scratch_shapes=[pltpu.VMEM(v.shape, v.dtype) for v in (grad, factor, sketch_ids)] + [pltpu.SemaphoreType.DMA((3,))],
        compiler_params=pltpu.CompilerParams(vmem_limit_bytes=56 << 20),
        cost_estimate=pl.CostEstimate(flops=10**8, bytes_accessed=4 * 10**6, transcendentals=0),
    )(grad, factor, sketch_ids)


def middle_kernel(at_ref, ranged_ref, grad_ref, factor_ref, part_ref):
    offset, mine, core = pl.multiple_of(at_ref[0], 16), at_ref[1], at_ref[2]
    wide, rows = grad_ref.shape[0], factor_ref.shape[0]
    ranged = ranged_ref[...]
    halves = [ranged[:, :LANES], ranged[:, LANES:]]
    moved = [pltpu.roll(v, 64, 1) for v in halves]
    low = lax.broadcasted_iota(jnp.int32, halves[0].shape, 1) < 64
    pick = jnp.where(core == 0, jnp.where(low, halves[0], moved[1]), jnp.where(low, moved[0], halves[1]))
    gram = dot(pick, ranged, 0, 0)
    here = jnp.where(mine == 1, ranged_ref[pl.ds(offset, rows), :], 0.0)
    weighted = sum(jnp.dot(grad_ref[...], v, preferred_element_type=F32) for v in split3(ranged))
    applied = decay_rate * dot(factor_ref[...], ranged, 1, 0)
    for k in range(NX):
        part_ref[k, :64, :] = gram[:64]
        part_ref[k, 64:96, :LANES] = gram[64:96, LANES:]
        part_ref[k, 64:96, LANES:] = gram[96:, LANES:]
        part_ref[k, 96:96 + rows, :] = here
        part_ref[k, 96 + rows:96 + rows + wide, :] = weighted
        part_ref[k, 96 + rows + wide:, :] = applied


def middle(at, ranged, grad, factor):
    whole = pl.BlockSpec(memory_space=pltpu.VMEM)
    return pl.pallas_call(
        middle_kernel,
        out_shape=jax.ShapeDtypeStruct((NX, 96 + 2 * factor.shape[0] + grad.shape[0], R), F32),
        in_specs=[pl.BlockSpec(memory_space=pltpu.SMEM)] + [whole] * 3,
        out_specs=whole,
        compiler_params=pltpu.CompilerParams(vmem_limit_bytes=24 << 20),
        cost_estimate=pl.CostEstimate(flops=10**8, bytes_accessed=4 * 10**6, transcendentals=0),
    )(at, ranged, grad, factor)


def shards(factor, gradient, sketch_ids):
    rows, cols = factor.shape
    z, y, c, x = (lax.axis_index(a) for a in ALL)
    owner = z // (NZ // NX)
    offset = rows * (((z % (NZ // NX)) * NY + y) * NC + c)
    mine = (x == owner).astype(F32)

    small, strip = front(gradient.T, factor, sketch_ids)
    plane = lax.all_gather(strip, ("z", "y"), axis=0, tiled=True)
    grad32 = gradient.astype(F32)
    small = jnp.sum(lax.all_to_all(small, "x", 0, 0), axis=0)
    inner, decayed = small[:gradient.shape[1]], small[gradient.shape[1]:]
    place = (lax.broadcasted_iota(jnp.int32, (cols, rows), 0) == offset + lax.broadcasted_iota(jnp.int32, (cols, rows), 1)).astype(F32)
    partial = dot(jnp.concatenate([grad32, mine * place], axis=1), jnp.concatenate([inner, decayed], axis=0), 1, 0)
    piece = scatter(scatter_core(partial, c), ("z", "y"), NZ * NY)
    piece = join(spread(piece, ("z", "y"), NZ * NY))
    ranged = lax.all_gather(piece, "c", axis=0, tiled=True)

    wide = gradient.shape[1]
    at = jnp.stack([offset, (x == owner).astype(jnp.int32), c])
    part = jnp.sum(lax.all_to_all(middle(at, ranged, gradient.T, factor), "x", 0, 0), axis=0)
    own_rows = part[96:96 + rows]
    left = part[96:96 + rows + wide]
    right = jnp.concatenate([part[96 + rows + wide:], part[96 + rows:96 + rows + wide]], axis=0)
    core = dot(left, right, 0, 0).reshape(NC, NX, 32, 256)
    core = lax.dynamic_index_in_dim(core, x, 1, keepdims=False).reshape(64, 256)
    both = lax.all_gather(jnp.concatenate([part[:96], core], axis=0), "c", axis=0, tiled=False)
    core = lax.dynamic_slice_in_dim(both[0, 96:] + both[1, 96:], 32 * c, 32, 0)
    inverse = inverse_factor(both, core)
    core = core_y = scatter(core, "y", NY)
    range_basis = dot(own_rows, inverse, 1, 1)
    core = after(jnp.sum(spread(core, "z", NZ), axis=0), range_basis)

    pair = 2 * rows
    start = offset - rows * c + nothing(range_basis)
    block = lax.dynamic_slice(plane, (0, start // LANES * LANES), (plane.shape[0], LANES))
    place = (lax.broadcasted_iota(jnp.int32, (LANES, pair), 0) == start % LANES + lax.broadcasted_iota(jnp.int32, (LANES, pair), 1))
    place = (place & (x == owner)).astype(BF16)
    picked = lax.dot_general(place, block, (((0,), (1,)), ((), ())), preferred_element_type=F32).astype(BF16)
    total = picked
    for k in range(1, NX):
        pairs = []
        for d in range(NZ * NY * NC):
            src = (d // (NY * NC)) // (NZ // NX)
            pairs.append((d * NX + src, d * NX + (src + k) % NX))
        total = total + lax.ppermute(picked, ALL, pairs)
    outer_sum = lax.dot_general(total, plane, (((1,), (0,)), ((), ())), preferred_element_type=F32)

    core = join(spread(core, ("x", "y"), NX * NY))
    other = lax.dynamic_slice_in_dim(outer_sum, (1 - c) * rows, rows, 0)
    both = lax.all_gather(jnp.concatenate([core] + [other[:, k:k + R] for k in range(0, cols, R)], axis=0), "c", axis=0, tiled=False)
    core = both[:, :128].reshape(R, R)
    other = lax.dynamic_index_in_dim(both[:, 128:], 1 - c, 0, keepdims=False)
    other = jnp.concatenate([other[k:k + rows] for k in range(0, other.shape[0], rows)], axis=1)
    factor_new = decay_rate * factor + (lax.dynamic_slice_in_dim(outer_sum, c * rows, rows, 0) + other)

    projected_core = dot(dot(inverse, core, 1, 0), inverse, 1, 1) / B
    return (factor_new, range_basis, projected_core)


def solution(mesh):
    fine = Mesh(mesh.devices.reshape(NZ, NY, NC, NX), ALL)
    f = ("z", "y", "c")
    return jax.shard_map(
        shards,
        mesh=fine,
        in_specs=(P(f, "x"), P("x", f), P("x", None)),
        out_specs=(P(f, "x"), P(f, None), P()),
        check_vma=False,
    )
```
